256 devices in a mesh: dom: 64 (over z, y, x_hi), col: 4 (over x_lo, core).
Axes of the slice: x: 4 (x_hi: 2, x_lo: 2; x = x_hi * 2 + x_lo), y: 4, z: 8, core: 2. Of those that a mesh axis runs over, the one named last changes fastest.
Arguments:
- embeddings: bfloat16 [2, 200, 262144], P(None, 'col', 'dom'), may hold values from -3 to 3
- relations: bfloat16 [2, 200, 512], P(None, 'col'), may hold values from -3 to 3
- source_ids: int32 [4, 65536], P(None, 'dom'), may hold values from 0 to 4095
- relation_ids: int32 [4, 65536], P(None, 'dom'), may hold values from 0 to 511
- target_ids: int32 [4, 65536], P(None, 'dom'), may hold values from 0 to 4095
- negative_ids: int32 [4, 256, 256], P(None, 'dom'), may hold values from 0 to 1023
- served_rows: int32 [4096, 16], P('dom'), may hold values from 0 to 4095
Outputs:
- entity_grad: float32 [2, 200, 262144], P(None, 'col', 'dom')
The draws below stay inside these ranges and needn't reach their ends.
All inputs are finite; a program needn't handle non-finite values.
Results may differ from the reference program's by a relative error of at most 0.007.
Values may be sent and summed in bfloat16 or wider, within the bound.
A program may use at most 128 MiB of HBM per device.

```python
import math
import jax
import jax.numpy as jnp
import numpy as np
from jax import lax

DIM = 200
RELS = 512
ENT_DEV = 4096
E_DEV = 1024
CH = 256
NCH = 256
NB = 4
CAP = 16
ENTS = 262144
EDGES = 65536
SPANS = 4
POOL = 1024
N_DOM = 64
N_COL = 4


def plant(entries, stream_key, smallest, top_value):
    longest = entries.shape.index(max(entries.shape))
    spots = []
    for shift in (0, 1):
        where = [jax.random.randint(jax.random.fold_in(stream_key, axis), (), 0, length) for axis, length in enumerate(entries.shape)]
        where[longest] = (where[longest] + shift) % entries.shape[longest]
        spots.append(tuple(where))
    return entries.at[spots[0]].set(smallest).at[spots[1]].set(top_value)


def level_of(own_key, shape, cuts, least, largest):
    factor_of, own = 1.0, jax.random.fold_in(own_key, 6)
    for dim, blocks in cuts:
        steps = jnp.exp(jax.random.uniform(jax.random.fold_in(own, dim), (blocks,), jnp.float32, least / len(cuts), largest / len(cuts)))
        factor_of = factor_of * jnp.repeat(steps, shape[dim] // blocks).reshape([-1 if axis == dim else 1 for axis in range(len(shape))])
    return factor_of


def rank_table(count, skew):
    loads = [(1 << 20) // math.isqrt(rank ** skew) + 1 for rank in range(1, count + 1)]
    spread = 1 + sum(loads) // (1 << 30)
    return np.cumsum(np.array([max(1, weight // spread) for weight in loads]))


def ranked_ids(stream_key, dims, number_of, slope):
    grid = rank_table(number_of, slope)
    lot = jax.random.randint(jax.random.fold_in(stream_key, 1), dims, 0, int(grid[number_of - 1]))
    grade = jnp.searchsorted(jnp.asarray(grid, jnp.int32), lot, side="right")
    return jax.random.permutation(jax.random.fold_in(stream_key, 2), number_of)[grade].astype(jnp.int32)


def gaussian(own_key, extent, deviation, bound, split=(), dtype=jnp.bfloat16):
    values = jax.random.normal(own_key, extent, jnp.float32) * deviation
    if len(split) > 0:
        values = level_of(own_key, extent, split, -0.22, 0.18) * values
    return jnp.clip(values, min=-bound, max=bound).astype(dtype)


def setup_inputs(seed: int = 0) -> dict:
    key_of = jax.random.split(jax.random.key(seed), 8)
    embeddings = gaussian(key_of[0], (2, DIM, ENTS), 0.5, 3.0, ((1, 4), (2, 64)))
    relations = gaussian(key_of[1], (2, DIM, RELS), 0.5, 3.0, ((1, 4),))
    source_ids = plant(jax.random.randint(key_of[2], (NB, EDGES), 0, ENT_DEV), jax.random.fold_in(key_of[2], 1), 0, ENT_DEV - 1).astype(jnp.int32)
    relation_ids = plant(ranked_ids(key_of[3], (NB, EDGES), RELS, 2), jax.random.fold_in(key_of[3], 3), 0, RELS - 1).astype(jnp.int32)
    target_ids = plant(ranked_ids(key_of[4], (NB, EDGES), ENT_DEV, 1), jax.random.fold_in(key_of[4], 3), 0, ENT_DEV - 1).astype(jnp.int32)
    negative_ids = plant(ranked_ids(key_of[5], (NB, SPANS * N_DOM, NCH), POOL, 1), jax.random.fold_in(key_of[5], 3), 0, POOL - 1).astype(jnp.int32)
    served_rows = plant(jax.random.randint(key_of[6], (N_DOM * N_DOM, CAP), 0, ENT_DEV), jax.random.fold_in(key_of[6], 1), 0, ENT_DEV - 1).astype(jnp.int32)
    return dict(embeddings=embeddings, relations=relations, source_ids=source_ids, relation_ids=relation_ids, target_ids=target_ids, negative_ids=negative_ids, served_rows=served_rows)


def partition_step(inputs):
    table_part, target_part, pool_part, sources, relation_rows, targets, negatives = inputs
    group_width = DIM // N_COL
    highest = lax.Precision.HIGHEST
    source_rows = table_part[:, :, sources].astype(jnp.float32)
    relation_vals = relation_rows.astype(jnp.float32)
    target_rows = target_part[:, :, targets].astype(jnp.float32)
    product = jnp.stack([source_rows[0] * relation_vals[0] - source_rows[1] * relation_vals[1],
                         source_rows[0] * relation_vals[1] + source_rows[1] * relation_vals[0]])
    rounded = lax.optimization_barrier(product.astype(jnp.bfloat16)).astype(jnp.float32)
    positive_cols = jnp.sum((rounded * target_rows).reshape(2, N_COL, group_width, E_DEV), axis=(0, 2))
    positive = jnp.sum(lax.optimization_barrier(positive_cols.astype(jnp.bfloat16)).astype(jnp.float32), axis=0)
    negative_rows = pool_part[:, :, negatives.reshape(-1)].astype(jnp.float32).reshape(2, DIM, SPANS, NCH)
    query_cols = rounded.reshape(2, N_COL, group_width, SPANS, CH)
    negative_groups = negative_rows.reshape(2, N_COL, group_width, SPANS, NCH)
    negative_cols = jnp.einsum('acdjh,acdjn->cjhn', query_cols, negative_groups, precision=highest)
    negative = jnp.sum(lax.optimization_barrier(negative_cols.astype(jnp.bfloat16)).astype(jnp.float32), axis=0)
    positive_slope = -jax.nn.sigmoid(-positive)
    negative_slope = lax.optimization_barrier(jax.nn.sigmoid(negative).astype(jnp.bfloat16)).astype(jnp.float32)
    query_rows = rounded.reshape(2, DIM, SPANS, CH)
    pool_terms = jnp.einsum('jhn,adjh->adjn', negative_slope, query_rows, precision=highest)
    pool_grad = jnp.zeros((2, DIM, POOL), jnp.float32).at[:, :, negatives.reshape(-1)].add(
        pool_terms.reshape(2, DIM, SPANS * NCH))
    query_terms = jnp.einsum('jhn,adjn->adjh', negative_slope, negative_rows, precision=highest).reshape(2, DIM, E_DEV)
    total = positive_slope * target_rows + query_terms
    source_grad = jnp.stack([total[0] * relation_vals[0] + total[1] * relation_vals[1],
                             total[1] * relation_vals[0] - total[0] * relation_vals[1]])
    source_full = jnp.zeros((2, DIM, ENT_DEV), jnp.float32).at[:, :, sources].add(source_grad)
    target_full = jnp.zeros((2, DIM, ENT_DEV), jnp.float32).at[:, :, targets].add(positive_slope * rounded)
    return source_full, target_full, pool_grad


def add_owned(gradient, indices, values):
    return gradient.at[:, :, indices].add(values)


def reference(embeddings, relations, source_ids, relation_ids, target_ids, negative_ids, served_rows):
    table = embeddings.reshape(2, DIM, N_DOM, ENT_DEV)
    served = served_rows.reshape(N_DOM, N_DOM * CAP)
    fetched = jnp.take_along_axis(table, served[None, None], axis=3)
    negative_pool = fetched.reshape(2, DIM, N_DOM, N_DOM, CAP).transpose(0, 1, 3, 2, 4).reshape(2, DIM, N_DOM, POOL)
    by_owner = jnp.moveaxis(table, 2, 0)
    pools = jnp.moveaxis(negative_pool, 2, 0)
    entity_sum = jnp.zeros((N_DOM, 2, DIM, ENT_DEV), jnp.float32)
    pool_sum = jnp.zeros((N_DOM, 2, DIM, POOL), jnp.float32)
    for bucket in range(NB):
        targets_block = jnp.roll(by_owner, bucket, axis=0)
        sources = source_ids[bucket].reshape(N_DOM, E_DEV)
        targets = target_ids[bucket].reshape(N_DOM, E_DEV)
        relation_rows = jnp.moveaxis(relations[:, :, relation_ids[bucket]].reshape(2, DIM, N_DOM, E_DEV), 2, 0)
        negatives = negative_ids[bucket].reshape(N_DOM, SPANS, NCH)
        source_terms, target_terms, pool_terms = lax.map(
            partition_step, (by_owner, targets_block, pools, sources, relation_rows, targets, negatives))
        entity_sum = entity_sum + source_terms + jnp.roll(target_terms, -bucket, axis=0)
        pool_sum = pool_sum + pool_terms
    returned = pool_sum.reshape(N_DOM, 2, DIM, N_DOM, CAP).transpose(3, 1, 2, 0, 4).reshape(N_DOM, 2, DIM, N_DOM * CAP)
    owned = jax.vmap(add_owned)(entity_sum, served, returned)
    return jnp.moveaxis(owned, 0, 2).reshape(2, DIM, ENTS)
```

```python
import jax
import jax.numpy as jnp
from jax import lax
from jax.sharding import PartitionSpec as P


def shifted(shard, axis, by):
    size = lax.axis_size(axis)
    return lax.ppermute(shard, axis, [(i, (i + by) % size) for i in range(size)])


def gather_cols(table, indices):
    count = table.shape[1]
    one_hot = (
        lax.broadcasted_iota(jnp.int32, (count, indices.shape[0]), 0) == indices[None, :]
    ).astype(table.dtype)
    return jnp.dot(table, one_hot, preferred_element_type=jnp.float32)


def split_exact(values):
    high = values.astype(jnp.bfloat16)
    low = (values - high.astype(jnp.float32)).astype(jnp.bfloat16)
    return high, low


def scatter_cols(values, indices, count):
    one_hot = (
        indices[:, None] == lax.broadcasted_iota(jnp.int32, (indices.shape[0], count), 1)
    ).astype(jnp.bfloat16)
    return jnp.dot(values, one_hot, preferred_element_type=jnp.float32)


def scatter_f32(values, indices, count):
    high, low = split_exact(values)
    return scatter_cols(
        jnp.concatenate([high, low], axis=1), jnp.concatenate([indices, indices]), count
    )


def body(embeddings, relations, source_ids, relation_ids, target_ids, negative_ids, served_rows):
    halves, columns, entities = embeddings.shape
    flat_width = halves * columns
    buckets, edge_count = source_ids.shape
    spans, negs_per = (negative_ids.shape[1], negative_ids.shape[2])
    span_len = edge_count // spans
    table = embeddings.reshape(flat_width, entities)
    relation_flat = relations.reshape(flat_width, relations.shape[2])
    served_flat = served_rows.reshape(-1)

    asked = [None] + [shifted(target_ids[b], "dom", -b) for b in range(1, buckets)]
    answered = [None] + [
        shifted(gather_cols(table, asked[b]).astype(jnp.bfloat16), "dom", b)
        for b in range(1, buckets)
    ]

    fetched = gather_cols(table, served_flat).astype(jnp.bfloat16)
    negative_pool = lax.all_to_all(
        fetched.reshape(halves, columns, -1), "dom", split_axis=2, concat_axis=2, tiled=True
    )
    pool_flat = negative_pool.reshape(flat_width, -1)
    pool_count = pool_flat.shape[1]

    def scores(bucket):
        negative_flat = negative_ids[bucket].reshape(-1)
        source_rows = gather_cols(table, source_ids[bucket]).reshape(halves, columns, edge_count)
        relation_rows = gather_cols(relation_flat, relation_ids[bucket]).reshape(
            halves, columns, edge_count
        )
        if bucket == 0:
            target_half = gather_cols(table, target_ids[0])
        else:
            target_half = answered[bucket].astype(jnp.float32)
        target_rows = target_half.reshape(halves, columns, edge_count)
        product = jnp.stack(
            [
                source_rows[0] * relation_rows[0] - source_rows[1] * relation_rows[1],
                source_rows[0] * relation_rows[1] + source_rows[1] * relation_rows[0],
            ]
        )
        rounded = product.astype(jnp.bfloat16)
        rounded_wide = rounded.astype(jnp.float32)
        positive_part = jnp.sum(rounded_wide * target_rows, axis=(0, 1))
        negative_rows = gather_cols(pool_flat, negative_flat).astype(jnp.bfloat16).reshape(
            flat_width, spans, negs_per
        )
        query_rows = rounded.reshape(flat_width, spans, span_len)
        negative_part = lax.dot_general(
            query_rows,
            negative_rows,
            (((0,), (0,)), ((1,), (1,))),
            preferred_element_type=jnp.float32,
        ).reshape(-1, 128)
        partial = jnp.concatenate(
            [negative_part, positive_part.reshape(-1, 128)], axis=0
        ).astype(jnp.bfloat16)
        state = (relation_rows, target_rows, rounded, rounded_wide, negative_rows, query_rows)
        return partial, state

    def gradients(bucket, reduced, state):
        relation_rows, target_rows, rounded, rounded_wide, negative_rows, query_rows = state
        reduced = reduced.astype(jnp.float32)
        negative = reduced[: edge_count * negs_per // 128].reshape(edge_count, negs_per)
        positive = reduced[edge_count * negs_per // 128 :].reshape(edge_count)
        positive_slope = -jax.nn.sigmoid(-positive)
        negative_slope = jax.nn.sigmoid(negative).astype(jnp.bfloat16)
        slope_spans = negative_slope.reshape(spans, span_len, negs_per)
        pool_terms = lax.dot_general(
            query_rows,
            slope_spans,
            (((2,), (1,)), ((1,), (0,))),
            preferred_element_type=jnp.float32,
        ).transpose(1, 0, 2).reshape(flat_width, spans * negs_per)
        query_terms = lax.dot_general(
            slope_spans,
            negative_rows,
            (((2,), (2,)), ((0,), (1,))),
            preferred_element_type=jnp.float32,
        )
        query_terms = query_terms.transpose(2, 0, 1).reshape(halves, columns, edge_count)
        total_grad = positive_slope * target_rows + query_terms
        target_values = (positive_slope * rounded_wide).reshape(flat_width, edge_count)
        source_grad = jnp.stack(
            [
                total_grad[0] * relation_rows[0] + total_grad[1] * relation_rows[1],
                total_grad[1] * relation_rows[0] - total_grad[0] * relation_rows[1],
            ]
        ).reshape(flat_width, edge_count)
        return pool_terms, target_values, source_grad

    owned = jnp.zeros((flat_width, entities), jnp.float32)
    pool_values, pool_index = [], []
    bf16_values, bf16_index = [], []
    previous = None
    for bucket in range(buckets + 1):
        current = None
        if bucket < buckets:
            partial, state = scores(bucket)
            if previous is not None:
                partial, prev_reduced = lax.optimization_barrier((partial, previous[1]))
                previous = (previous[0], prev_reduced, previous[2])
            current = (bucket, lax.psum(partial, "col"), state)
        if previous is not None:
            done, reduced, state = previous
            pool_terms, target_values, source_grad = gradients(done, reduced, state)
            pool_values.append(pool_terms)
            pool_index.append(negative_ids[done].reshape(-1))
            if done == 0:
                owned = owned + scatter_f32(
                    jnp.concatenate([source_grad, target_values], axis=1),
                    jnp.concatenate([source_ids[0], target_ids[0]]),
                    entities,
                )
            else:
                owned = owned + scatter_f32(source_grad, source_ids[done], entities)
                bf16_values.append(shifted(target_values.astype(jnp.bfloat16), "dom", -done))
                bf16_index.append(asked[done])
        previous = current

    pool_grad = scatter_f32(
        jnp.concatenate(pool_values, axis=1), jnp.concatenate(pool_index), pool_count
    )
    returned = lax.all_to_all(
        pool_grad.reshape(halves, columns, -1).astype(jnp.bfloat16),
        "dom",
        split_axis=2,
        concat_axis=2,
        tiled=True,
    ).reshape(flat_width, -1)
    bf16_values.append(returned)
    bf16_index.append(served_flat)
    owned = owned + scatter_cols(
        jnp.concatenate(bf16_values, axis=1), jnp.concatenate(bf16_index), entities
    )
    return owned.reshape(halves, columns, entities)


def solution(mesh):
    placed = (
        P(None, "col", "dom"),
        P(None, "col", None),
        P(None, "dom"),
        P(None, "dom"),
        P(None, "dom"),
        P(None, "dom", None),
        P("dom", None),
    )
    return jax.shard_map(
        body, mesh=mesh, in_specs=placed, out_specs=P(None, "col", "dom"), check_vma=False
    )
```

```python
import functools

import jax
import jax.numpy as jnp
from jax import lax
from jax.experimental import pallas as pl
from jax.experimental.pallas import tpu as pltpu
from jax.sharding import PartitionSpec as P

MESH_ID = pl.DeviceIdType.MESH


def exchange_kernel(parts, neg_rows, partial_ref, neg_out, pos_out,
                    received, slopes, sums, send_a, recv_a, send_b, recv_b, send_c, recv_c):
    me = lax.axis_index("col")
    dom = lax.axis_index("dom")
    others = [lax.rem(me + d, parts) for d in range(1, parts)]

    barrier = pltpu.get_barrier_semaphore()
    for other in others:
        pl.semaphore_signal(barrier, inc=1, device_id=(dom, other), device_id_type=MESH_ID)
    pl.semaphore_wait(barrier, parts - 1)

    def first(src, dst):
        return pltpu.make_async_remote_copy(
            src_ref=partial_ref.at[dst], dst_ref=received.at[src],
            send_sem=send_a.at[dst], recv_sem=recv_a.at[src],
            device_id=(dom, dst), device_id_type=MESH_ID)

    outgoing = [first(me, other) for other in others]
    for copy in outgoing:
        copy.start()
    for other in others:
        first(other, me).wait_recv()
    for copy in outgoing:
        copy.wait_send()

    total = partial_ref[me].astype(jnp.float32)
    for other in others:
        total = total + received[other].astype(jnp.float32)
    slopes[me] = (1.0 / (1.0 + jnp.exp(-total[:neg_rows]))).astype(slopes.dtype)
    sums[me] = total[neg_rows:neg_rows + 8]

    def second(src, dst):
        return (
            pltpu.make_async_remote_copy(
                src_ref=slopes.at[src], dst_ref=slopes.at[src],
                send_sem=send_b.at[dst], recv_sem=recv_b.at[src],
                device_id=(dom, dst), device_id_type=MESH_ID),
            pltpu.make_async_remote_copy(
                src_ref=sums.at[src], dst_ref=sums.at[src],
                send_sem=send_c.at[dst], recv_sem=recv_c.at[src],
                device_id=(dom, dst), device_id_type=MESH_ID),
        )

    outgoing = [c for other in others for c in second(me, other)]
    for copy in outgoing:
        copy.start()
    for other in others:
        for copy in second(other, me):
            copy.wait_recv()
    for copy in outgoing:
        copy.wait_send()
    neg_out[...] = slopes[...]
    pos_out[...] = sums[...]


def col_exchange(partial, bucket):
    parts, rows, lanes = partial.shape
    neg_rows = rows - 16
    vmem = pl.BlockSpec(memory_space=pltpu.VMEM)
    return pl.pallas_call(
        functools.partial(exchange_kernel, parts, neg_rows),
        out_shape=(
            jax.ShapeDtypeStruct((parts, neg_rows, lanes), jnp.bfloat16),
            jax.ShapeDtypeStruct((parts, 8, lanes), jnp.float32),
        ),
        in_specs=[vmem],
        out_specs=(vmem, vmem),
        scratch_shapes=[
            pltpu.VMEM((parts, rows, lanes), jnp.bfloat16),
            pltpu.VMEM((parts, neg_rows, lanes), jnp.bfloat16),
            pltpu.VMEM((parts, 8, lanes), jnp.float32),
        ] + [pltpu.SemaphoreType.DMA((parts,))] * 6,
        compiler_params=pltpu.CompilerParams(collective_id=bucket, has_side_effects=True),
    )(partial)


def shifted(shard, axis, by):
    size = lax.axis_size(axis)
    return lax.ppermute(shard, axis, [(i, (i + by) % size) for i in range(size)])


def gather_cols(table, indices):
    count = table.shape[1]
    one_hot = (
        lax.broadcasted_iota(jnp.int32, (count, indices.shape[0]), 0) == indices[None, :]
    ).astype(table.dtype)
    return jnp.dot(table, one_hot, preferred_element_type=jnp.float32)


def split_exact(values):
    high = values.astype(jnp.bfloat16)
    low = (values - high.astype(jnp.float32)).astype(jnp.bfloat16)
    return high, low


def scatter_cols(values, indices, count):
    one_hot = (
        indices[:, None] == lax.broadcasted_iota(jnp.int32, (indices.shape[0], count), 1)
    ).astype(jnp.bfloat16)
    return jnp.dot(values, one_hot, preferred_element_type=jnp.float32)


def scatter_f32(values, indices, count):
    high, low = split_exact(values)
    return scatter_cols(
        jnp.concatenate([high, low], axis=1), jnp.concatenate([indices, indices]), count
    )


def body(embeddings, relations, source_ids, relation_ids, target_ids, negative_ids, served_rows):
    halves, columns, entities = embeddings.shape
    flat_width = halves * columns
    buckets, edge_count = source_ids.shape
    spans, negs_per = (negative_ids.shape[1], negative_ids.shape[2])
    span_len = edge_count // spans
    table = embeddings.reshape(flat_width, entities)
    relation_flat = relations.reshape(flat_width, relations.shape[2])
    served_flat = served_rows.reshape(-1)

    asked = [None] + [shifted(target_ids[b], "dom", -b) for b in range(1, buckets)]
    answered = [None] + [
        shifted(gather_cols(table, asked[b]).astype(jnp.bfloat16), "dom", b)
        for b in range(1, buckets)
    ]

    fetched = gather_cols(table, served_flat).astype(jnp.bfloat16)
    negative_pool = lax.all_to_all(
        fetched.reshape(halves, columns, -1), "dom", split_axis=2, concat_axis=2, tiled=True
    )
    pool_flat = negative_pool.reshape(flat_width, -1)
    pool_count = pool_flat.shape[1]

    def scores(bucket):
        negative_flat = negative_ids[bucket].reshape(-1)
        source_rows = gather_cols(table, source_ids[bucket]).reshape(halves, columns, edge_count)
        relation_rows = gather_cols(relation_flat, relation_ids[bucket]).reshape(
            halves, columns, edge_count
        )
        if bucket == 0:
            target_half = gather_cols(table, target_ids[0])
        else:
            target_half = answered[bucket].astype(jnp.float32)
        target_rows = target_half.reshape(halves, columns, edge_count)
        product = jnp.stack(
            [
                source_rows[0] * relation_rows[0] - source_rows[1] * relation_rows[1],
                source_rows[0] * relation_rows[1] + source_rows[1] * relation_rows[0],
            ]
        )
        rounded = product.astype(jnp.bfloat16)
        rounded_wide = rounded.astype(jnp.float32)
        positive_part = jnp.sum(rounded_wide * target_rows, axis=(0, 1))
        negative_rows = gather_cols(pool_flat, negative_flat).astype(jnp.bfloat16).reshape(
            flat_width, spans, negs_per
        )
        query_rows = rounded.reshape(flat_width, spans, span_len)
        negative_part = lax.dot_general(
            query_rows,
            negative_rows,
            (((0,), (0,)), ((1,), (1,))),
            preferred_element_type=jnp.float32,
        ).reshape(spans, -1, 128)
        positive_rows = positive_part.reshape(spans, -1, 128)
        pad = jnp.zeros((spans, 16 - positive_rows.shape[1], 128), jnp.float32)
        partial = jnp.concatenate([negative_part, positive_rows, pad], axis=1).astype(
            jnp.bfloat16
        )
        state = (relation_rows, target_rows, rounded, rounded_wide, negative_rows, query_rows)
        return partial, state

    def gradients(bucket, reduced, state):
        relation_rows, target_rows, rounded, rounded_wide, negative_rows, query_rows = state
        negative_slope, positive_sums = reduced
        positive = positive_sums[:, : span_len // 128].reshape(edge_count)
        positive_slope = -jax.nn.sigmoid(-positive)
        slope_spans = negative_slope.reshape(spans, span_len, negs_per)
        pool_terms = lax.dot_general(
            query_rows,
            slope_spans,
            (((2,), (1,)), ((1,), (0,))),
            preferred_element_type=jnp.float32,
        ).transpose(1, 0, 2).reshape(flat_width, spans * negs_per)
        query_terms = lax.dot_general(
            slope_spans,
            negative_rows,
            (((2,), (2,)), ((0,), (1,))),
            preferred_element_type=jnp.float32,
        )
        query_terms = query_terms.transpose(2, 0, 1).reshape(halves, columns, edge_count)
        total_grad = positive_slope * target_rows + query_terms
        target_values = (positive_slope * rounded_wide).reshape(flat_width, edge_count)
        source_grad = jnp.stack(
            [
                total_grad[0] * relation_rows[0] + total_grad[1] * relation_rows[1],
                total_grad[1] * relation_rows[0] - total_grad[0] * relation_rows[1],
            ]
        ).reshape(flat_width, edge_count)
        return pool_terms, target_values, source_grad

    owned = jnp.zeros((flat_width, entities), jnp.float32)
    pool_values, pool_index = [], []
    bf16_values, bf16_index = [], []
    previous = None
    for bucket in range(buckets + 1):
        current = None
        if bucket < buckets:
            partial, state = scores(bucket)
            if previous is not None:
                partial, prev_reduced = lax.optimization_barrier((partial, previous[1]))
                previous = (previous[0], prev_reduced, previous[2])
            current = (bucket, col_exchange(partial, bucket), state)
        if previous is not None:
            done, reduced, state = previous
            pool_terms, target_values, source_grad = gradients(done, reduced, state)
            pool_values.append(pool_terms)
            pool_index.append(negative_ids[done].reshape(-1))
            if done == 0:
                owned = owned + scatter_f32(
                    jnp.concatenate([source_grad, target_values], axis=1),
                    jnp.concatenate([source_ids[0], target_ids[0]]),
                    entities,
                )
            else:
                owned = owned + scatter_f32(source_grad, source_ids[done], entities)
                bf16_values.append(shifted(target_values.astype(jnp.bfloat16), "dom", -done))
                bf16_index.append(asked[done])
        previous = current

    pool_grad = scatter_f32(
        jnp.concatenate(pool_values, axis=1), jnp.concatenate(pool_index), pool_count
    )
    returned = lax.all_to_all(
        pool_grad.reshape(halves, columns, -1).astype(jnp.bfloat16),
        "dom",
        split_axis=2,
        concat_axis=2,
        tiled=True,
    ).reshape(flat_width, -1)
    bf16_values.append(returned)
    bf16_index.append(served_flat)
    owned = owned + scatter_cols(
        jnp.concatenate(bf16_values, axis=1), jnp.concatenate(bf16_index), entities
    )
    return owned.reshape(halves, columns, entities)


def solution(mesh):
    placed = (
        P(None, "col", "dom"),
        P(None, "col", None),
        P(None, "dom"),
        P(None, "dom"),
        P(None, "dom"),
        P(None, "dom", None),
        P("dom", None),
    )
    return jax.shard_map(
        body, mesh=mesh, in_specs=placed, out_specs=P(None, "col", "dom"), check_vma=False
    )
```

```python
import functools

import jax
import jax.numpy as jnp
from jax import lax
from jax.experimental import pallas as pl
from jax.experimental.pallas import tpu as pltpu
from jax.sharding import PartitionSpec as P

MESH_ID = pl.DeviceIdType.MESH


def exchange_kernel(parts, neg_rows, partial_ref, neg_out, pos_out,
                    received, slopes, sums, send_a, recv_a, send_b, recv_b, send_c, recv_c):
    me = lax.axis_index("col")
    dom = lax.axis_index("dom")
    others = [lax.rem(me + d, parts) for d in range(1, parts)]

    barrier = pltpu.get_barrier_semaphore()
    for other in others:
        pl.semaphore_signal(barrier, inc=1, device_id=(dom, other), device_id_type=MESH_ID)
    pl.semaphore_wait(barrier, parts - 1)

    def first(src, dst):
        return pltpu.make_async_remote_copy(
            src_ref=partial_ref.at[dst], dst_ref=received.at[src],
            send_sem=send_a.at[dst], recv_sem=recv_a.at[src],
            device_id=(dom, dst), device_id_type=MESH_ID)

    outgoing = [first(me, other) for other in others]
    for copy in outgoing:
        copy.start()
    for other in others:
        first(other, me).wait_recv()
    for copy in outgoing:
        copy.wait_send()

    total = partial_ref[me].astype(jnp.float32)
    for other in others:
        total = total + received[other].astype(jnp.float32)
    slopes[me] = (1.0 / (1.0 + jnp.exp(-total[:neg_rows]))).astype(slopes.dtype)
    sums[me] = total[neg_rows:neg_rows + 8]

    def second(src, dst):
        return (
            pltpu.make_async_remote_copy(
                src_ref=slopes.at[src], dst_ref=slopes.at[src],
                send_sem=send_b.at[dst], recv_sem=recv_b.at[src],
                device_id=(dom, dst), device_id_type=MESH_ID),
            pltpu.make_async_remote_copy(
                src_ref=sums.at[src], dst_ref=sums.at[src],
                send_sem=send_c.at[dst], recv_sem=recv_c.at[src],
                device_id=(dom, dst), device_id_type=MESH_ID),
        )

    outgoing = [c for other in others for c in second(me, other)]
    for copy in outgoing:
        copy.start()
    for other in others:
        for copy in second(other, me):
            copy.wait_recv()
    for copy in outgoing:
        copy.wait_send()
    neg_out[...] = slopes[...]
    pos_out[...] = sums[...]


def col_exchange(partial, bucket):
    parts, rows, lanes = partial.shape
    neg_rows = rows - 16
    vmem = pl.BlockSpec(memory_space=pltpu.VMEM)
    return pl.pallas_call(
        functools.partial(exchange_kernel, parts, neg_rows),
        out_shape=(
            jax.ShapeDtypeStruct((parts, neg_rows, lanes), jnp.bfloat16),
            jax.ShapeDtypeStruct((parts, 8, lanes), jnp.float32),
        ),
        in_specs=[vmem],
        out_specs=(vmem, vmem),
        scratch_shapes=[
            pltpu.VMEM((parts, rows, lanes), jnp.bfloat16),
            pltpu.VMEM((parts, neg_rows, lanes), jnp.bfloat16),
            pltpu.VMEM((parts, 8, lanes), jnp.float32),
        ] + [pltpu.SemaphoreType.DMA((parts,))] * 6,
        compiler_params=pltpu.CompilerParams(collective_id=bucket, has_side_effects=True),
    )(partial)


def shifted(shard, axis, by):
    size = lax.axis_size(axis)
    return lax.ppermute(shard, axis, [(i, (i + by) % size) for i in range(size)])


def gather_cols(table, indices):
    count = table.shape[1]
    one_hot = (
        lax.broadcasted_iota(jnp.int32, (count, indices.shape[0]), 0) == indices[None, :]
    ).astype(table.dtype)
    return jnp.dot(table, one_hot, preferred_element_type=jnp.float32)


def split_exact(values):
    high = values.astype(jnp.bfloat16)
    low = (values - high.astype(jnp.float32)).astype(jnp.bfloat16)
    return high, low


def scatter_cols(values, indices, count):
    one_hot = (
        indices[:, None] == lax.broadcasted_iota(jnp.int32, (indices.shape[0], count), 1)
    ).astype(jnp.bfloat16)
    return jnp.dot(values, one_hot, preferred_element_type=jnp.float32)


def scatter_f32(values, indices, count):
    rows = values.shape[0]
    high, low = split_exact(values)
    summed = scatter_cols(jnp.concatenate([high, low], axis=0), indices, count)
    return summed[:rows] + summed[rows:]


def body(embeddings, relations, source_ids, relation_ids, target_ids, negative_ids, served_rows):
    halves, columns, entities = embeddings.shape
    flat_width = halves * columns
    buckets, edge_count = source_ids.shape
    spans, negs_per = (negative_ids.shape[1], negative_ids.shape[2])
    span_len = edge_count // spans
    table = embeddings.reshape(flat_width, entities)
    relation_flat = relations.reshape(flat_width, relations.shape[2])
    served_flat = served_rows.reshape(-1)

    asked = [None] + [shifted(target_ids[b], "dom", -b) for b in range(1, buckets)]
    answered = [None] + [
        shifted(gather_cols(table, asked[b]).astype(jnp.bfloat16), "dom", b)
        for b in range(1, buckets)
    ]

    fetched = gather_cols(table, served_flat).astype(jnp.bfloat16)
    negative_pool = lax.all_to_all(
        fetched.reshape(halves, columns, -1), "dom", split_axis=2, concat_axis=2, tiled=True
    )
    pool_flat = negative_pool.reshape(flat_width, -1)
    pool_count = pool_flat.shape[1]

    def scores(bucket):
        negative_flat = negative_ids[bucket].reshape(-1)
        source_rows = gather_cols(table, source_ids[bucket]).reshape(halves, columns, edge_count)
        relation_rows = gather_cols(relation_flat, relation_ids[bucket]).reshape(
            halves, columns, edge_count
        )
        if bucket == 0:
            target_half = gather_cols(table, target_ids[0])
        else:
            target_half = answered[bucket].astype(jnp.float32)
        target_rows = target_half.reshape(halves, columns, edge_count)
        product = jnp.stack(
            [
                source_rows[0] * relation_rows[0] - source_rows[1] * relation_rows[1],
                source_rows[0] * relation_rows[1] + source_rows[1] * relation_rows[0],
            ]
        )
        rounded = product.astype(jnp.bfloat16)
        rounded_wide = rounded.astype(jnp.float32)
        positive_part = jnp.sum(rounded_wide * target_rows, axis=(0, 1))
        negative_rows = gather_cols(pool_flat, negative_flat).astype(jnp.bfloat16).reshape(
            flat_width, spans, negs_per
        )
        query_rows = rounded.reshape(flat_width, spans, span_len)
        negative_part = lax.dot_general(
            query_rows,
            negative_rows,
            (((0,), (0,)), ((1,), (1,))),
            preferred_element_type=jnp.float32,
        ).reshape(spans, -1, 128)
        positive_rows = positive_part.reshape(spans, -1, 128)
        pad = jnp.zeros((spans, 16 - positive_rows.shape[1], 128), jnp.float32)
        partial = jnp.concatenate([negative_part, positive_rows, pad], axis=1).astype(
            jnp.bfloat16
        )
        state = (relation_rows, target_rows, rounded, rounded_wide, negative_rows, query_rows)
        return partial, state

    def gradients(bucket, reduced, state):
        relation_rows, target_rows, rounded, rounded_wide, negative_rows, query_rows = state
        negative_slope, positive_sums = reduced
        positive = positive_sums[:, : span_len // 128].reshape(edge_count)
        positive_slope = -jax.nn.sigmoid(-positive)
        slope_spans = negative_slope.reshape(spans, span_len, negs_per)
        pool_terms = lax.dot_general(
            query_rows,
            slope_spans,
            (((2,), (1,)), ((1,), (0,))),
            preferred_element_type=jnp.float32,
        ).transpose(1, 0, 2).reshape(flat_width, spans * negs_per)
        query_terms = lax.dot_general(
            slope_spans,
            negative_rows,
            (((2,), (2,)), ((0,), (1,))),
            preferred_element_type=jnp.float32,
        )
        query_terms = query_terms.transpose(2, 0, 1).reshape(halves, columns, edge_count)
        total_grad = positive_slope * target_rows + query_terms
        target_values = (positive_slope * rounded_wide).reshape(flat_width, edge_count)
        source_grad = jnp.stack(
            [
                total_grad[0] * relation_rows[0] + total_grad[1] * relation_rows[1],
                total_grad[1] * relation_rows[0] - total_grad[0] * relation_rows[1],
            ]
        ).reshape(flat_width, edge_count)
        return pool_terms, target_values, source_grad

    owned = jnp.zeros((flat_width, entities), jnp.float32)
    pool_values, pool_index = [], []
    bf16_values, bf16_index = [], []
    previous = None
    for bucket in range(buckets + 1):
        current = None
        if bucket < buckets:
            partial, state = scores(bucket)
            if previous is not None:
                partial, prev_reduced = lax.optimization_barrier((partial, previous[1]))
                previous = (previous[0], prev_reduced, previous[2])
            current = (bucket, col_exchange(partial, bucket), state)
        if previous is not None:
            done, reduced, state = previous
            pool_terms, target_values, source_grad = gradients(done, reduced, state)
            pool_values.append(pool_terms)
            pool_index.append(negative_ids[done].reshape(-1))
            if done == 0:
                owned = owned + scatter_f32(
                    jnp.concatenate([source_grad, target_values], axis=1),
                    jnp.concatenate([source_ids[0], target_ids[0]]),
                    entities,
                )
            else:
                owned = owned + scatter_f32(source_grad, source_ids[done], entities)
                bf16_values.append(shifted(target_values.astype(jnp.bfloat16), "dom", -done))
                bf16_index.append(asked[done])
        previous = current

    pool_grad = scatter_f32(
        jnp.concatenate(pool_values, axis=1), jnp.concatenate(pool_index), pool_count
    )
    returned = lax.all_to_all(
        pool_grad.reshape(halves, columns, -1).astype(jnp.bfloat16),
        "dom",
        split_axis=2,
        concat_axis=2,
        tiled=True,
    ).reshape(flat_width, -1)
    bf16_values.append(returned)
    bf16_index.append(served_flat)
    owned = owned + scatter_cols(
        jnp.concatenate(bf16_values, axis=1), jnp.concatenate(bf16_index), entities
    )
    return owned.reshape(halves, columns, entities)


def solution(mesh):
    placed = (
        P(None, "col", "dom"),
        P(None, "col", None),
        P(None, "dom"),
        P(None, "dom"),
        P(None, "dom"),
        P(None, "dom", None),
        P("dom", None),
    )
    return jax.shard_map(
        body, mesh=mesh, in_specs=placed, out_specs=P(None, "col", "dom"), check_vma=False
    )
```

```python
import functools

import jax
import jax.numpy as jnp
from jax import lax
from jax.experimental import pallas as pl
from jax.experimental.pallas import tpu as pltpu
from jax.sharding import PartitionSpec as P

MESH_ID = pl.DeviceIdType.MESH


def exchange_kernel(parts, batches, neg_rows, partial_ref, neg_out, pos_out,
                    received, slopes, sums, send_a, recv_a, send_b, recv_b, send_c, recv_c):
    me = lax.axis_index("col")
    dom = lax.axis_index("dom")
    others = [lax.rem(me + d, parts) for d in range(1, parts)]

    barrier = pltpu.get_barrier_semaphore()
    for other in others:
        pl.semaphore_signal(barrier, inc=1, device_id=(dom, other), device_id_type=MESH_ID)
    pl.semaphore_wait(barrier, parts - 1)

    def first(batch, src, dst):
        return pltpu.make_async_remote_copy(
            src_ref=partial_ref.at[dst, batch], dst_ref=received.at[src, batch],
            send_sem=send_a.at[batch * parts + dst], recv_sem=recv_a.at[batch * parts + src],
            device_id=(dom, dst), device_id_type=MESH_ID)

    def second(batch, src, dst):
        return (
            pltpu.make_async_remote_copy(
                src_ref=slopes.at[src, batch], dst_ref=slopes.at[src, batch],
                send_sem=send_b.at[batch * parts + dst], recv_sem=recv_b.at[batch * parts + src],
                device_id=(dom, dst), device_id_type=MESH_ID),
            pltpu.make_async_remote_copy(
                src_ref=sums.at[src, batch], dst_ref=sums.at[src, batch],
                send_sem=send_c.at[batch * parts + dst], recv_sem=recv_c.at[batch * parts + src],
                device_id=(dom, dst), device_id_type=MESH_ID),
        )

    outgoing = [first(batch, me, other) for batch in range(batches) for other in others]
    for copy in outgoing:
        copy.start()
    returning = []
    for batch in range(batches):
        for other in others:
            first(batch, other, me).wait_recv()
        total = partial_ref[me, batch].astype(jnp.float32)
        for other in others:
            total = total + received[other, batch].astype(jnp.float32)
        slopes[me, batch] = (1.0 / (1.0 + jnp.exp(-total[:neg_rows]))).astype(slopes.dtype)
        sums[me, batch] = total[neg_rows:neg_rows + 8]
        copies = [c for other in others for c in second(batch, me, other)]
        for copy in copies:
            copy.start()
        returning += copies
    for copy in outgoing:
        copy.wait_send()
    for batch in range(batches):
        for other in others:
            for copy in second(batch, other, me):
                copy.wait_recv()
    for copy in returning:
        copy.wait_send()
    neg_out[...] = slopes[...]
    pos_out[...] = sums[...]


def col_exchange(partial):
    parts, batches, rows, lanes = partial.shape
    neg_rows = rows - 16
    vmem = pl.BlockSpec(memory_space=pltpu.VMEM)
    return pl.pallas_call(
        functools.partial(exchange_kernel, parts, batches, neg_rows),
        out_shape=(
            jax.ShapeDtypeStruct((parts, batches, neg_rows, lanes), jnp.bfloat16),
            jax.ShapeDtypeStruct((parts, batches, 8, lanes), jnp.float32),
        ),
        in_specs=[vmem],
        out_specs=(vmem, vmem),
        scratch_shapes=[
            pltpu.VMEM((parts, batches, rows, lanes), jnp.bfloat16),
            pltpu.VMEM((parts, batches, neg_rows, lanes), jnp.bfloat16),
            pltpu.VMEM((parts, batches, 8, lanes), jnp.float32),
        ] + [pltpu.SemaphoreType.DMA((parts * batches,))] * 6,
        compiler_params=pltpu.CompilerParams(
            collective_id=0, has_side_effects=True, vmem_limit_bytes=48 * 1024 * 1024
        ),
    )(partial)


def shifted(shard, axis, by):
    size = lax.axis_size(axis)
    return lax.ppermute(shard, axis, [(i, (i + by) % size) for i in range(size)])


def gather_cols(table, indices):
    count = table.shape[1]
    one_hot = (
        lax.broadcasted_iota(jnp.int32, (count, indices.shape[0]), 0) == indices[None, :]
    ).astype(table.dtype)
    return jnp.dot(table, one_hot, preferred_element_type=jnp.float32)


def split_exact(values):
    high = values.astype(jnp.bfloat16)
    low = (values - high.astype(jnp.float32)).astype(jnp.bfloat16)
    return high, low


def scatter_cols(values, indices, count):
    one_hot = (
        indices[:, None] == lax.broadcasted_iota(jnp.int32, (indices.shape[0], count), 1)
    ).astype(jnp.bfloat16)
    return jnp.dot(values, one_hot, preferred_element_type=jnp.float32)


def scatter_f32(values, indices, count):
    rows = values.shape[0]
    high, low = split_exact(values)
    summed = scatter_cols(jnp.concatenate([high, low], axis=0), indices, count)
    return summed[:rows] + summed[rows:]


def body(embeddings, relations, source_ids, relation_ids, target_ids, negative_ids, served_rows):
    halves, columns, entities = embeddings.shape
    flat_width = halves * columns
    buckets, edge_count = source_ids.shape
    spans, negs_per = (negative_ids.shape[1], negative_ids.shape[2])
    span_len = edge_count // spans
    table = embeddings.reshape(flat_width, entities)
    relation_flat = relations.reshape(flat_width, relations.shape[2])
    served_flat = served_rows.reshape(-1)

    asked = [None] + [shifted(target_ids[b], "dom", -b) for b in range(1, buckets)]
    answered = [None] + [
        shifted(gather_cols(table, asked[b]).astype(jnp.bfloat16), "dom", b)
        for b in range(1, buckets)
    ]

    fetched = gather_cols(table, served_flat).astype(jnp.bfloat16)
    negative_pool = lax.all_to_all(
        fetched.reshape(halves, columns, -1), "dom", split_axis=2, concat_axis=2, tiled=True
    )
    pool_flat = negative_pool.reshape(flat_width, -1)
    pool_count = pool_flat.shape[1]

    def scores(bucket):
        negative_flat = negative_ids[bucket].reshape(-1)
        source_rows = gather_cols(table, source_ids[bucket]).reshape(halves, columns, edge_count)
        relation_rows = gather_cols(relation_flat, relation_ids[bucket]).reshape(
            halves, columns, edge_count
        )
        if bucket == 0:
            target_half = gather_cols(table, target_ids[0])
        else:
            target_half = answered[bucket].astype(jnp.float32)
        target_rows = target_half.reshape(halves, columns, edge_count)
        product = jnp.stack(
            [
                source_rows[0] * relation_rows[0] - source_rows[1] * relation_rows[1],
                source_rows[0] * relation_rows[1] + source_rows[1] * relation_rows[0],
            ]
        )
        rounded = product.astype(jnp.bfloat16)
        rounded_wide = rounded.astype(jnp.float32)
        positive_part = jnp.sum(rounded_wide * target_rows, axis=(0, 1))
        negative_rows = gather_cols(pool_flat, negative_flat).astype(jnp.bfloat16).reshape(
            flat_width, spans, negs_per
        )
        query_rows = rounded.reshape(flat_width, spans, span_len)
        negative_part = lax.dot_general(
            query_rows,
            negative_rows,
            (((0,), (0,)), ((1,), (1,))),
            preferred_element_type=jnp.float32,
        ).reshape(spans, -1, 128)
        positive_rows = positive_part.reshape(spans, -1, 128)
        pad = jnp.zeros((spans, 16 - positive_rows.shape[1], 128), jnp.float32)
        partial = jnp.concatenate([negative_part, positive_rows, pad], axis=1).astype(
            jnp.bfloat16
        )
        state = (relation_rows, target_rows, rounded, rounded_wide, negative_rows, query_rows)
        return partial, state

    def gradients(bucket, reduced, state):
        relation_rows, target_rows, rounded, rounded_wide, negative_rows, query_rows = state
        negative_slope, positive_sums = reduced
        positive = positive_sums[:, : span_len // 128].reshape(edge_count)
        positive_slope = -jax.nn.sigmoid(-positive)
        slope_spans = negative_slope.reshape(spans, span_len, negs_per)
        pool_terms = lax.dot_general(
            query_rows,
            slope_spans,
            (((2,), (1,)), ((1,), (0,))),
            preferred_element_type=jnp.float32,
        ).transpose(1, 0, 2).reshape(flat_width, spans * negs_per)
        query_terms = lax.dot_general(
            slope_spans,
            negative_rows,
            (((2,), (2,)), ((0,), (1,))),
            preferred_element_type=jnp.float32,
        )
        query_terms = query_terms.transpose(2, 0, 1).reshape(halves, columns, edge_count)
        total_grad = positive_slope * target_rows + query_terms
        target_values = (positive_slope * rounded_wide).reshape(flat_width, edge_count)
        source_grad = jnp.stack(
            [
                total_grad[0] * relation_rows[0] + total_grad[1] * relation_rows[1],
                total_grad[1] * relation_rows[0] - total_grad[0] * relation_rows[1],
            ]
        ).reshape(flat_width, edge_count)
        return pool_terms, target_values, source_grad

    owned = jnp.zeros((flat_width, entities), jnp.float32)
    pool_values, pool_index = [], []
    bf16_values, bf16_index = [], []
    results = [scores(bucket) for bucket in range(buckets)]
    negative_all, positive_all = col_exchange(jnp.stack([r[0] for r in results], axis=1))
    for done in range(buckets):
        reduced = (negative_all[:, done], positive_all[:, done])
        pool_terms, target_values, source_grad = gradients(done, reduced, results[done][1])
        pool_values.append(pool_terms)
        pool_index.append(negative_ids[done].reshape(-1))
        if done == 0:
            owned = owned + scatter_f32(
                jnp.concatenate([source_grad, target_values], axis=1),
                jnp.concatenate([source_ids[0], target_ids[0]]),
                entities,
            )
        else:
            owned = owned + scatter_f32(source_grad, source_ids[done], entities)
            bf16_values.append(shifted(target_values.astype(jnp.bfloat16), "dom", -done))
            bf16_index.append(asked[done])

    pool_grad = scatter_f32(
        jnp.concatenate(pool_values, axis=1), jnp.concatenate(pool_index), pool_count
    )
    returned = lax.all_to_all(
        pool_grad.reshape(halves, columns, -1).astype(jnp.bfloat16),
        "dom",
        split_axis=2,
        concat_axis=2,
        tiled=True,
    ).reshape(flat_width, -1)
    bf16_values.append(returned)
    bf16_index.append(served_flat)
    owned = owned + scatter_cols(
        jnp.concatenate(bf16_values, axis=1), jnp.concatenate(bf16_index), entities
    )
    return owned.reshape(halves, columns, entities)


def solution(mesh):
    placed = (
        P(None, "col", "dom"),
        P(None, "col", None),
        P(None, "dom"),
        P(None, "dom"),
        P(None, "dom"),
        P(None, "dom", None),
        P("dom", None),
    )
    return jax.shard_map(
        body, mesh=mesh, in_specs=placed, out_specs=P(None, "col", "dom"), check_vma=False
    )
```

```python
import functools

import jax
import jax.numpy as jnp
from jax import lax
from jax.experimental import pallas as pl
from jax.experimental.pallas import tpu as pltpu
from jax.sharding import PartitionSpec as P

MESH_ID = pl.DeviceIdType.MESH


def exchange_kernel(parts, batches, neg_rows, partial_ref, neg_out, pos_out,
                    received, slopes, sums, send_a, recv_a, send_b, recv_b, send_c, recv_c):
    me = lax.axis_index("col")
    dom = lax.axis_index("dom")
    others = [lax.rem(me + d, parts) for d in range(1, parts)]

    barrier = pltpu.get_barrier_semaphore()
    for other in others:
        pl.semaphore_signal(barrier, inc=1, device_id=(dom, other), device_id_type=MESH_ID)
    pl.semaphore_wait(barrier, parts - 1)

    def first(batch, src, dst):
        return pltpu.make_async_remote_copy(
            src_ref=partial_ref.at[dst, batch], dst_ref=received.at[src, batch],
            send_sem=send_a.at[batch * parts + dst], recv_sem=recv_a.at[batch * parts + src],
            device_id=(dom, dst), device_id_type=MESH_ID)

    def second(batch, src, dst):
        return (
            pltpu.make_async_remote_copy(
                src_ref=slopes.at[src, batch], dst_ref=slopes.at[src, batch],
                send_sem=send_b.at[batch * parts + dst], recv_sem=recv_b.at[batch * parts + src],
                device_id=(dom, dst), device_id_type=MESH_ID),
            pltpu.make_async_remote_copy(
                src_ref=sums.at[src, batch], dst_ref=sums.at[src, batch],
                send_sem=send_c.at[batch * parts + dst], recv_sem=recv_c.at[batch * parts + src],
                device_id=(dom, dst), device_id_type=MESH_ID),
        )

    outgoing = [first(batch, me, other) for batch in range(batches) for other in others]
    for copy in outgoing:
        copy.start()
    returning = []
    for batch in range(batches):
        for other in others:
            first(batch, other, me).wait_recv()
        total = partial_ref[me, batch].astype(jnp.float32)
        for other in others:
            total = total + received[other, batch].astype(jnp.float32)
        slopes[me, batch] = (1.0 / (1.0 + jnp.exp(-total[:neg_rows]))).astype(slopes.dtype)
        sums[me, batch] = total[neg_rows:neg_rows + 8]
        copies = [c for other in others for c in second(batch, me, other)]
        for copy in copies:
            copy.start()
        returning += copies
    for copy in outgoing:
        copy.wait_send()
    for batch in range(batches):
        for other in others:
            for copy in second(batch, other, me):
                copy.wait_recv()
    for copy in returning:
        copy.wait_send()
    neg_out[...] = slopes[...]
    pos_out[...] = sums[...]


def col_exchange(partial):
    parts, batches, rows, lanes = partial.shape
    neg_rows = rows - 16
    vmem = pl.BlockSpec(memory_space=pltpu.VMEM)
    return pl.pallas_call(
        functools.partial(exchange_kernel, parts, batches, neg_rows),
        out_shape=(
            jax.ShapeDtypeStruct((parts, batches, neg_rows, lanes), jnp.bfloat16),
            jax.ShapeDtypeStruct((parts, batches, 8, lanes), jnp.float32),
        ),
        in_specs=[vmem],
        out_specs=(vmem, vmem),
        scratch_shapes=[
            pltpu.VMEM((parts, batches, rows, lanes), jnp.bfloat16),
            pltpu.VMEM((parts, batches, neg_rows, lanes), jnp.bfloat16),
            pltpu.VMEM((parts, batches, 8, lanes), jnp.float32),
        ] + [pltpu.SemaphoreType.DMA((parts * batches,))] * 6,
        compiler_params=pltpu.CompilerParams(
            collective_id=0, has_side_effects=True, vmem_limit_bytes=48 * 1024 * 1024
        ),
    )(partial)


def shifted(shard, axis, by):
    size = lax.axis_size(axis)
    return lax.ppermute(shard, axis, [(i, (i + by) % size) for i in range(size)])


def gather_cols(table, indices):
    count = table.shape[1]
    one_hot = (
        lax.broadcasted_iota(jnp.int32, (count, indices.shape[0]), 0) == indices[None, :]
    ).astype(table.dtype)
    return jnp.dot(table, one_hot, preferred_element_type=jnp.float32)


def split_exact(values):
    high = values.astype(jnp.bfloat16)
    low = (values - high.astype(jnp.float32)).astype(jnp.bfloat16)
    return high, low


def scatter_rows(values, indices, count):
    one_hot = (
        lax.broadcasted_iota(jnp.int32, (count, indices.shape[0]), 0) == indices[None, :]
    ).astype(jnp.bfloat16)
    return lax.dot_general(
        one_hot, values, (((1,), (1,)), ((), ())), preferred_element_type=jnp.float32
    )


def scatter_f32(values, indices, count):
    rows = values.shape[0]
    high, low = split_exact(values)
    summed = scatter_rows(jnp.concatenate([high, low], axis=0), indices, count)
    return summed[:, :rows] + summed[:, rows:]


def body(embeddings, relations, source_ids, relation_ids, target_ids, negative_ids, served_rows):
    halves, columns, entities = embeddings.shape
    flat_width = halves * columns
    buckets, edge_count = source_ids.shape
    spans, negs_per = (negative_ids.shape[1], negative_ids.shape[2])
    span_len = edge_count // spans
    table = embeddings.reshape(flat_width, entities)
    relation_flat = relations.reshape(flat_width, relations.shape[2])
    served_flat = served_rows.reshape(-1)

    asked = [None] + [shifted(target_ids[b], "dom", -b) for b in range(1, buckets)]
    answered = [None] + [
        shifted(gather_cols(table, asked[b]).astype(jnp.bfloat16), "dom", b)
        for b in range(1, buckets)
    ]

    fetched = gather_cols(table, served_flat).astype(jnp.bfloat16)
    negative_pool = lax.all_to_all(
        fetched.reshape(halves, columns, -1), "dom", split_axis=2, concat_axis=2, tiled=True
    )
    pool_flat = negative_pool.reshape(flat_width, -1)
    pool_count = pool_flat.shape[1]

    def scores(bucket):
        negative_flat = negative_ids[bucket].reshape(-1)
        source_rows = gather_cols(table, source_ids[bucket]).reshape(halves, columns, edge_count)
        relation_rows = gather_cols(relation_flat, relation_ids[bucket]).reshape(
            halves, columns, edge_count
        )
        if bucket == 0:
            target_half = gather_cols(table, target_ids[0])
        else:
            target_half = answered[bucket].astype(jnp.float32)
        target_rows = target_half.reshape(halves, columns, edge_count)
        product = jnp.stack(
            [
                source_rows[0] * relation_rows[0] - source_rows[1] * relation_rows[1],
                source_rows[0] * relation_rows[1] + source_rows[1] * relation_rows[0],
            ]
        )
        rounded = product.astype(jnp.bfloat16)
        rounded_wide = rounded.astype(jnp.float32)
        positive_part = jnp.sum(rounded_wide * target_rows, axis=(0, 1))
        negative_rows = gather_cols(pool_flat, negative_flat).astype(jnp.bfloat16).reshape(
            flat_width, spans, negs_per
        )
        query_rows = rounded.reshape(flat_width, spans, span_len)
        negative_part = lax.dot_general(
            query_rows,
            negative_rows,
            (((0,), (0,)), ((1,), (1,))),
            preferred_element_type=jnp.float32,
        ).reshape(spans, -1, 128)
        positive_rows = positive_part.reshape(spans, -1, 128)
        pad = jnp.zeros((spans, 16 - positive_rows.shape[1], 128), jnp.float32)
        partial = jnp.concatenate([negative_part, positive_rows, pad], axis=1).astype(
            jnp.bfloat16
        )
        state = (relation_rows, target_rows, rounded, rounded_wide, negative_rows, query_rows)
        return partial, state

    def gradients(bucket, reduced, state):
        relation_rows, target_rows, rounded, rounded_wide, negative_rows, query_rows = state
        negative_slope, positive_sums = reduced
        positive = positive_sums[:, : span_len // 128].reshape(edge_count)
        positive_slope = -jax.nn.sigmoid(-positive)
        slope_spans = negative_slope.reshape(spans, span_len, negs_per)
        pool_terms = lax.dot_general(
            query_rows,
            slope_spans,
            (((2,), (1,)), ((1,), (0,))),
            preferred_element_type=jnp.float32,
        ).transpose(1, 0, 2).reshape(flat_width, spans * negs_per)
        query_terms = lax.dot_general(
            slope_spans,
            negative_rows,
            (((2,), (2,)), ((0,), (1,))),
            preferred_element_type=jnp.float32,
        )
        query_terms = query_terms.transpose(2, 0, 1).reshape(halves, columns, edge_count)
        total_grad = positive_slope * target_rows + query_terms
        target_values = (positive_slope * rounded_wide).reshape(flat_width, edge_count)
        source_grad = jnp.stack(
            [
                total_grad[0] * relation_rows[0] + total_grad[1] * relation_rows[1],
                total_grad[1] * relation_rows[0] - total_grad[0] * relation_rows[1],
            ]
        ).reshape(flat_width, edge_count)
        return pool_terms, target_values, source_grad

    owned = jnp.zeros((entities, flat_width), jnp.float32)
    pool_values, pool_index = [], []
    bf16_values, bf16_index = [], []
    results = [scores(bucket) for bucket in range(buckets)]
    negative_all, positive_all = col_exchange(jnp.stack([r[0] for r in results], axis=1))
    for done in range(buckets):
        reduced = (negative_all[:, done], positive_all[:, done])
        pool_terms, target_values, source_grad = gradients(done, reduced, results[done][1])
        pool_values.append(pool_terms)
        pool_index.append(negative_ids[done].reshape(-1))
        if done == 0:
            owned = owned + scatter_f32(
                jnp.concatenate([source_grad, target_values], axis=1),
                jnp.concatenate([source_ids[0], target_ids[0]]),
                entities,
            )
        else:
            owned = owned + scatter_f32(source_grad, source_ids[done], entities)
            bf16_values.append(shifted(target_values.astype(jnp.bfloat16), "dom", -done))
            bf16_index.append(asked[done])

    pool_grad = scatter_f32(
        jnp.concatenate(pool_values, axis=1), jnp.concatenate(pool_index), pool_count
    ).T
    returned = lax.all_to_all(
        pool_grad.reshape(halves, columns, -1).astype(jnp.bfloat16),
        "dom",
        split_axis=2,
        concat_axis=2,
        tiled=True,
    ).reshape(flat_width, -1)
    bf16_values.append(returned)
    bf16_index.append(served_flat)
    owned = owned + scatter_rows(
        jnp.concatenate(bf16_values, axis=1), jnp.concatenate(bf16_index), entities
    )
    return owned.T.reshape(halves, columns, entities)


def solution(mesh):
    placed = (
        P(None, "col", "dom"),
        P(None, "col", None),
        P(None, "dom"),
        P(None, "dom"),
        P(None, "dom"),
        P(None, "dom", None),
        P("dom", None),
    )
    return jax.shard_map(
        body, mesh=mesh, in_specs=placed, out_specs=P(None, "col", "dom"), check_vma=False
    )
```

```python
import functools

import jax
import jax.numpy as jnp
from jax import lax
from jax.experimental import pallas as pl
from jax.experimental.pallas import tpu as pltpu
from jax.sharding import PartitionSpec as P

MESH_ID = pl.DeviceIdType.MESH


def exchange_kernel(batches, neg_rows, partial_ref, neg_out, pos_out,
                    received, crossing, arrived, slopes, sums,
                    send_a, recv_a, send_x, recv_x, send_b, recv_b, send_c, recv_c):
    me = lax.axis_index("col")
    dom = lax.axis_index("dom")
    pair = me + 1 - 2 * lax.rem(me, 2)
    cross = lax.rem(me + 2, 4)
    far = lax.rem(pair + 2, 4)

    barrier = pltpu.get_barrier_semaphore()
    for other in (pair, cross):
        pl.semaphore_signal(barrier, inc=1, device_id=(dom, other), device_id_type=MESH_ID)
    pl.semaphore_wait(barrier, 2)

    def on_chip(batch, slot, span):
        return pltpu.make_async_remote_copy(
            src_ref=partial_ref.at[span, batch], dst_ref=received.at[slot, batch],
            send_sem=send_a.at[batch * 2 + slot], recv_sem=recv_a.at[batch * 2 + slot],
            device_id=(dom, pair), device_id_type=MESH_ID)

    def across(batch):
        return pltpu.make_async_remote_copy(
            src_ref=crossing.at[batch], dst_ref=arrived.at[batch],
            send_sem=send_x.at[batch], recv_sem=recv_x.at[batch],
            device_id=(dom, cross), device_id_type=MESH_ID)

    def slope_copies(batch, span, dst, route):
        return (
            pltpu.make_async_remote_copy(
                src_ref=slopes.at[span, batch], dst_ref=slopes.at[span, batch],
                send_sem=send_b.at[batch * 3 + route], recv_sem=recv_b.at[batch * 4 + span],
                device_id=(dom, dst), device_id_type=MESH_ID),
            pltpu.make_async_remote_copy(
                src_ref=sums.at[span, batch], dst_ref=sums.at[span, batch],
                send_sem=send_c.at[batch * 3 + route], recv_sem=recv_c.at[batch * 4 + span],
                device_id=(dom, dst), device_id_type=MESH_ID),
        )

    started = []
    for batch in range(batches):
        for copy in (on_chip(batch, 0, pair), on_chip(batch, 1, far)):
            copy.start()
            started.append(copy)
    for batch in range(batches):
        on_chip(batch, 0, me).wait_recv()
        on_chip(batch, 1, cross).wait_recv()
        crossing[batch] = (
            partial_ref[cross, batch].astype(jnp.float32) + received[1, batch].astype(jnp.float32)
        ).astype(crossing.dtype)
        copy = across(batch)
        copy.start()
        started.append(copy)
    for batch in range(batches):
        across(batch).wait_recv()
        total = (
            partial_ref[me, batch].astype(jnp.float32)
            + received[0, batch].astype(jnp.float32)
            + arrived[batch].astype(jnp.float32)
        )
        slopes[me, batch] = (1.0 / (1.0 + jnp.exp(-total[:neg_rows]))).astype(slopes.dtype)
        sums[me, batch] = total[neg_rows:neg_rows + 8]
        for copy in slope_copies(batch, me, cross, 0) + slope_copies(batch, me, pair, 1):
            copy.start()
            started.append(copy)
    for batch in range(batches):
        for copy in slope_copies(batch, cross, me, 0):
            copy.wait_recv()
        for copy in slope_copies(batch, cross, pair, 2):
            copy.start()
            started.append(copy)
    for batch in range(batches):
        for copy in slope_copies(batch, pair, me, 1) + slope_copies(batch, far, me, 2):
            copy.wait_recv()
    for copy in started:
        copy.wait_send()
    neg_out[...] = slopes[...]
    pos_out[...] = sums[...]


def col_exchange(partial):
    parts, batches, rows, lanes = partial.shape
    neg_rows = rows - 16
    vmem = pl.BlockSpec(memory_space=pltpu.VMEM)
    return pl.pallas_call(
        functools.partial(exchange_kernel, batches, neg_rows),
        out_shape=(
            jax.ShapeDtypeStruct((parts, batches, neg_rows, lanes), jnp.bfloat16),
            jax.ShapeDtypeStruct((parts, batches, 8, lanes), jnp.float32),
        ),
        in_specs=[vmem],
        out_specs=(vmem, vmem),
        scratch_shapes=[
            pltpu.VMEM((2, batches, rows, lanes), jnp.bfloat16),
            pltpu.VMEM((batches, rows, lanes), jnp.bfloat16),
            pltpu.VMEM((batches, rows, lanes), jnp.bfloat16),
            pltpu.VMEM((parts, batches, neg_rows, lanes), jnp.bfloat16),
            pltpu.VMEM((parts, batches, 8, lanes), jnp.float32),
            pltpu.SemaphoreType.DMA((2 * batches,)),
            pltpu.SemaphoreType.DMA((2 * batches,)),
            pltpu.SemaphoreType.DMA((batches,)),
            pltpu.SemaphoreType.DMA((batches,)),
            pltpu.SemaphoreType.DMA((3 * batches,)),
            pltpu.SemaphoreType.DMA((parts * batches,)),
            pltpu.SemaphoreType.DMA((3 * batches,)),
            pltpu.SemaphoreType.DMA((parts * batches,)),
        ],
        compiler_params=pltpu.CompilerParams(
            collective_id=0, has_side_effects=True, vmem_limit_bytes=48 * 1024 * 1024
        ),
    )(partial)


def shifted(shard, axis, by):
    size = lax.axis_size(axis)
    return lax.ppermute(shard, axis, [(i, (i + by) % size) for i in range(size)])


def gather_cols(table, indices):
    count = table.shape[1]
    one_hot = (
        lax.broadcasted_iota(jnp.int32, (count, indices.shape[0]), 0) == indices[None, :]
    ).astype(table.dtype)
    return jnp.dot(table, one_hot, preferred_element_type=jnp.float32)


def split_exact(values):
    high = values.astype(jnp.bfloat16)
    low = (values - high.astype(jnp.float32)).astype(jnp.bfloat16)
    return high, low


def scatter_rows(values, indices, count):
    one_hot = (
        lax.broadcasted_iota(jnp.int32, (count, indices.shape[0]), 0) == indices[None, :]
    ).astype(jnp.bfloat16)
    return lax.dot_general(
        one_hot, values, (((1,), (1,)), ((), ())), preferred_element_type=jnp.float32
    )


def scatter_f32(values, indices, count):
    rows = values.shape[0]
    high, low = split_exact(values)
    summed = scatter_rows(jnp.concatenate([high, low], axis=0), indices, count)
    return summed[:, :rows] + summed[:, rows:]


def body(embeddings, relations, source_ids, relation_ids, target_ids, negative_ids, served_rows):
    halves, columns, entities = embeddings.shape
    flat_width = halves * columns
    buckets, edge_count = source_ids.shape
    spans, negs_per = (negative_ids.shape[1], negative_ids.shape[2])
    span_len = edge_count // spans
    table = embeddings.reshape(flat_width, entities)
    relation_flat = relations.reshape(flat_width, relations.shape[2])
    served_flat = served_rows.reshape(-1)

    asked = [None] + [shifted(target_ids[b], "dom", -b) for b in range(1, buckets)]
    answered = [None] + [
        shifted(gather_cols(table, asked[b]).astype(jnp.bfloat16), "dom", b)
        for b in range(1, buckets)
    ]

    fetched = gather_cols(table, served_flat).astype(jnp.bfloat16)
    negative_pool = lax.all_to_all(
        fetched.reshape(halves, columns, -1), "dom", split_axis=2, concat_axis=2, tiled=True
    )
    pool_flat = negative_pool.reshape(flat_width, -1)
    pool_count = pool_flat.shape[1]

    def scores(bucket):
        negative_flat = negative_ids[bucket].reshape(-1)
        source_rows = gather_cols(table, source_ids[bucket]).reshape(halves, columns, edge_count)
        relation_rows = gather_cols(relation_flat, relation_ids[bucket]).reshape(
            halves, columns, edge_count
        )
        if bucket == 0:
            target_half = gather_cols(table, target_ids[0])
        else:
            target_half = answered[bucket].astype(jnp.float32)
        target_rows = target_half.reshape(halves, columns, edge_count)
        product = jnp.stack(
            [
                source_rows[0] * relation_rows[0] - source_rows[1] * relation_rows[1],
                source_rows[0] * relation_rows[1] + source_rows[1] * relation_rows[0],
            ]
        )
        rounded = product.astype(jnp.bfloat16)
        rounded_wide = rounded.astype(jnp.float32)
        positive_part = jnp.sum(rounded_wide * target_rows, axis=(0, 1))
        negative_rows = gather_cols(pool_flat, negative_flat).astype(jnp.bfloat16).reshape(
            flat_width, spans, negs_per
        )
        query_rows = rounded.reshape(flat_width, spans, span_len)
        negative_part = lax.dot_general(
            query_rows,
            negative_rows,
            (((0,), (0,)), ((1,), (1,))),
            preferred_element_type=jnp.float32,
        ).reshape(spans, -1, 128)
        positive_rows = positive_part.reshape(spans, -1, 128)
        pad = jnp.zeros((spans, 16 - positive_rows.shape[1], 128), jnp.float32)
        partial = jnp.concatenate([negative_part, positive_rows, pad], axis=1).astype(
            jnp.bfloat16
        )
        state = (relation_rows, target_rows, rounded, rounded_wide, negative_rows, query_rows)
        return partial, state

    def gradients(bucket, reduced, state):
        relation_rows, target_rows, rounded, rounded_wide, negative_rows, query_rows = state
        negative_slope, positive_sums = reduced
        positive = positive_sums[:, : span_len // 128].reshape(edge_count)
        positive_slope = -jax.nn.sigmoid(-positive)
        slope_spans = negative_slope.reshape(spans, span_len, negs_per)
        pool_terms = lax.dot_general(
            query_rows,
            slope_spans,
            (((2,), (1,)), ((1,), (0,))),
            preferred_element_type=jnp.float32,
        ).transpose(1, 0, 2).reshape(flat_width, spans * negs_per)
        query_terms = lax.dot_general(
            slope_spans,
            negative_rows,
            (((2,), (2,)), ((0,), (1,))),
            preferred_element_type=jnp.float32,
        )
        query_terms = query_terms.transpose(2, 0, 1).reshape(halves, columns, edge_count)
        total_grad = positive_slope * target_rows + query_terms
        target_values = (positive_slope * rounded_wide).reshape(flat_width, edge_count)
        source_grad = jnp.stack(
            [
                total_grad[0] * relation_rows[0] + total_grad[1] * relation_rows[1],
                total_grad[1] * relation_rows[0] - total_grad[0] * relation_rows[1],
            ]
        ).reshape(flat_width, edge_count)
        return pool_terms, target_values, source_grad

    owned = jnp.zeros((entities, flat_width), jnp.float32)
    pool_values, pool_index = [], []
    bf16_values, bf16_index = [], []
    results = [scores(bucket) for bucket in range(buckets)]
    negative_all, positive_all = col_exchange(jnp.stack([r[0] for r in results], axis=1))
    for done in range(buckets):
        reduced = (negative_all[:, done], positive_all[:, done])
        pool_terms, target_values, source_grad = gradients(done, reduced, results[done][1])
        pool_values.append(pool_terms)
        pool_index.append(negative_ids[done].reshape(-1))
        if done == 0:
            owned = owned + scatter_f32(
                jnp.concatenate([source_grad, target_values], axis=1),
                jnp.concatenate([source_ids[0], target_ids[0]]),
                entities,
            )
        else:
            owned = owned + scatter_f32(source_grad, source_ids[done], entities)
            bf16_values.append(shifted(target_values.astype(jnp.bfloat16), "dom", -done))
            bf16_index.append(asked[done])

    pool_grad = scatter_f32(
        jnp.concatenate(pool_values, axis=1), jnp.concatenate(pool_index), pool_count
    ).T
    returned = lax.all_to_all(
        pool_grad.reshape(halves, columns, -1).astype(jnp.bfloat16),
        "dom",
        split_axis=2,
        concat_axis=2,
        tiled=True,
    ).reshape(flat_width, -1)
    bf16_values.append(returned)
    bf16_index.append(served_flat)
    owned = owned + scatter_rows(
        jnp.concatenate(bf16_values, axis=1), jnp.concatenate(bf16_index), entities
    )
    return owned.T.reshape(halves, columns, entities)


def solution(mesh):
    placed = (
        P(None, "col", "dom"),
        P(None, "col", None),
        P(None, "dom"),
        P(None, "dom"),
        P(None, "dom"),
        P(None, "dom", None),
        P("dom", None),
    )
    return jax.shard_map(
        body, mesh=mesh, in_specs=placed, out_specs=P(None, "col", "dom"), check_vma=False
    )
```

```python
import functools

import jax
import jax.numpy as jnp
from jax import lax
from jax.experimental import pallas as pl
from jax.experimental.pallas import tpu as pltpu
from jax.sharding import PartitionSpec as P

MESH_ID = pl.DeviceIdType.MESH


def exchange_kernel(batches, neg_rows, partial_ref, neg_out, pos_out,
                    received, crossing, arrived, slopes, sums,
                    send_a, recv_a, send_x, recv_x, send_b, recv_b, send_c, recv_c):
    me = lax.axis_index("col")
    dom = lax.axis_index("dom")
    pair = me + 1 - 2 * lax.rem(me, 2)
    cross = lax.rem(me + 2, 4)
    far = lax.rem(pair + 2, 4)

    barrier = pltpu.get_barrier_semaphore()
    for other in (pair, cross):
        pl.semaphore_signal(barrier, inc=1, device_id=(dom, other), device_id_type=MESH_ID)
    pl.semaphore_wait(barrier, 2)

    def on_chip(batch, slot, span):
        return pltpu.make_async_remote_copy(
            src_ref=partial_ref.at[span, batch], dst_ref=received.at[slot, batch],
            send_sem=send_a.at[batch * 2 + slot], recv_sem=recv_a.at[batch * 2 + slot],
            device_id=(dom, pair), device_id_type=MESH_ID)

    def across(batch):
        return pltpu.make_async_remote_copy(
            src_ref=crossing.at[batch], dst_ref=arrived.at[batch],
            send_sem=send_x.at[batch], recv_sem=recv_x.at[batch],
            device_id=(dom, cross), device_id_type=MESH_ID)

    def slope_copies(batch, span, dst, route):
        return (
            pltpu.make_async_remote_copy(
                src_ref=slopes.at[span, batch], dst_ref=slopes.at[span, batch],
                send_sem=send_b.at[batch * 3 + route], recv_sem=recv_b.at[batch * 4 + span],
                device_id=(dom, dst), device_id_type=MESH_ID),
            pltpu.make_async_remote_copy(
                src_ref=sums.at[span, batch], dst_ref=sums.at[span, batch],
                send_sem=send_c.at[batch * 3 + route], recv_sem=recv_c.at[batch * 4 + span],
                device_id=(dom, dst), device_id_type=MESH_ID),
        )

    started = []
    for batch in range(batches):
        for copy in (on_chip(batch, 0, pair), on_chip(batch, 1, far)):
            copy.start()
            started.append(copy)
    for batch in range(batches):
        on_chip(batch, 0, me).wait_recv()
        on_chip(batch, 1, cross).wait_recv()
        crossing[batch] = (
            partial_ref[cross, batch].astype(jnp.float32) + received[1, batch].astype(jnp.float32)
        ).astype(crossing.dtype)
        copy = across(batch)
        copy.start()
        started.append(copy)
    for batch in range(batches):
        across(batch).wait_recv()
        total = (
            partial_ref[me, batch].astype(jnp.float32)
            + received[0, batch].astype(jnp.float32)
            + arrived[batch].astype(jnp.float32)
        )
        slopes[me, batch] = (1.0 / (1.0 + jnp.exp(-total[:neg_rows]))).astype(slopes.dtype)
        sums[me, batch] = total[neg_rows:neg_rows + 8]
        for copy in slope_copies(batch, me, cross, 0) + slope_copies(batch, me, pair, 1):
            copy.start()
            started.append(copy)
    for batch in range(batches):
        for copy in slope_copies(batch, cross, me, 0):
            copy.wait_recv()
        for copy in slope_copies(batch, cross, pair, 2):
            copy.start()
            started.append(copy)
    for batch in range(batches):
        for copy in slope_copies(batch, pair, me, 1) + slope_copies(batch, far, me, 2):
            copy.wait_recv()
    for copy in started:
        copy.wait_send()
    neg_out[...] = slopes[...]
    pos_out[...] = sums[...]


def col_exchange(partial):
    parts, batches, rows, lanes = partial.shape
    neg_rows = rows - 16
    vmem = pl.BlockSpec(memory_space=pltpu.VMEM)
    return pl.pallas_call(
        functools.partial(exchange_kernel, batches, neg_rows),
        out_shape=(
            jax.ShapeDtypeStruct((parts, batches, neg_rows, lanes), jnp.bfloat16),
            jax.ShapeDtypeStruct((parts, batches, 8, lanes), jnp.float32),
        ),
        in_specs=[vmem],
        out_specs=(vmem, vmem),
        scratch_shapes=[
            pltpu.VMEM((2, batches, rows, lanes), jnp.bfloat16),
            pltpu.VMEM((batches, rows, lanes), jnp.bfloat16),
            pltpu.VMEM((batches, rows, lanes), jnp.bfloat16),
            pltpu.VMEM((parts, batches, neg_rows, lanes), jnp.bfloat16),
            pltpu.VMEM((parts, batches, 8, lanes), jnp.float32),
            pltpu.SemaphoreType.DMA((2 * batches,)),
            pltpu.SemaphoreType.DMA((2 * batches,)),
            pltpu.SemaphoreType.DMA((batches,)),
            pltpu.SemaphoreType.DMA((batches,)),
            pltpu.SemaphoreType.DMA((3 * batches,)),
            pltpu.SemaphoreType.DMA((parts * batches,)),
            pltpu.SemaphoreType.DMA((3 * batches,)),
            pltpu.SemaphoreType.DMA((parts * batches,)),
        ],
        compiler_params=pltpu.CompilerParams(
            collective_id=0, has_side_effects=True, vmem_limit_bytes=48 * 1024 * 1024
        ),
    )(partial)


def scatter_kernel(count, tile, ids_ref, values_ref, out_ref):
    width = ids_ref.shape[1]
    out_ref[...] = jnp.zeros_like(out_ref)

    def per_tile(block, carry):
        first = pl.multiple_of(block * tile, tile)
        rows = lax.broadcasted_iota(jnp.int32, (tile, tile), 0) + first

        def per_chunk(chunk, inner):
            start = pl.multiple_of(chunk * tile, tile)
            one_hot = (rows == ids_ref[:, pl.ds(start, tile)]).astype(values_ref.dtype)
            out_ref[pl.ds(first, tile), :] += jnp.dot(
                one_hot, values_ref[pl.ds(start, tile), :], preferred_element_type=jnp.float32
            )
            return inner

        return lax.fori_loop(0, width // tile, per_chunk, carry)

    lax.fori_loop(0, count // tile, per_tile, 0)


def scatter_pallas(values_t, indices, count):
    tile = 256
    vmem = pl.BlockSpec(memory_space=pltpu.VMEM)
    return pl.pallas_call(
        functools.partial(scatter_kernel, count, tile),
        out_shape=jax.ShapeDtypeStruct((count, values_t.shape[1]), jnp.float32),
        in_specs=[vmem, vmem],
        out_specs=vmem,
        compiler_params=pltpu.CompilerParams(vmem_limit_bytes=48 * 1024 * 1024),
    )(indices.reshape(1, -1), values_t)


def padded_t(values, width):
    rows = values.shape[0]
    return jnp.pad(values, ((0, width - rows), (0, 0))).T


def shifted(shard, axis, by):
    size = lax.axis_size(axis)
    return lax.ppermute(shard, axis, [(i, (i + by) % size) for i in range(size)])


def gather_cols(table, indices):
    count = table.shape[1]
    one_hot = (
        lax.broadcasted_iota(jnp.int32, (count, indices.shape[0]), 0) == indices[None, :]
    ).astype(table.dtype)
    return jnp.dot(table, one_hot, preferred_element_type=jnp.float32)


def split_exact(values):
    high = values.astype(jnp.bfloat16)
    low = (values - high.astype(jnp.float32)).astype(jnp.bfloat16)
    return high, low


def scatter_rows(values, indices, count):
    one_hot = (
        lax.broadcasted_iota(jnp.int32, (count, indices.shape[0]), 0) == indices[None, :]
    ).astype(jnp.bfloat16)
    return lax.dot_general(
        one_hot, values, (((1,), (1,)), ((), ())), preferred_element_type=jnp.float32
    )


def scatter_f32(values, indices, count):
    rows = values.shape[0]
    high, low = split_exact(values)
    summed = scatter_rows(jnp.concatenate([high, low], axis=0), indices, count)
    return summed[:, :rows] + summed[:, rows:]


def body(embeddings, relations, source_ids, relation_ids, target_ids, negative_ids, served_rows):
    halves, columns, entities = embeddings.shape
    flat_width = halves * columns
    buckets, edge_count = source_ids.shape
    spans, negs_per = (negative_ids.shape[1], negative_ids.shape[2])
    span_len = edge_count // spans
    table = embeddings.reshape(flat_width, entities)
    relation_flat = relations.reshape(flat_width, relations.shape[2])
    served_flat = served_rows.reshape(-1)

    asked = [None] + [shifted(target_ids[b], "dom", -b) for b in range(1, buckets)]
    answered = [None] + [
        shifted(gather_cols(table, asked[b]).astype(jnp.bfloat16), "dom", b)
        for b in range(1, buckets)
    ]

    fetched = gather_cols(table, served_flat).astype(jnp.bfloat16)
    negative_pool = lax.all_to_all(
        fetched.reshape(halves, columns, -1), "dom", split_axis=2, concat_axis=2, tiled=True
    )
    pool_flat = negative_pool.reshape(flat_width, -1)
    pool_count = pool_flat.shape[1]

    def scores(bucket):
        negative_flat = negative_ids[bucket].reshape(-1)
        source_rows = gather_cols(table, source_ids[bucket]).reshape(halves, columns, edge_count)
        relation_rows = gather_cols(relation_flat, relation_ids[bucket]).reshape(
            halves, columns, edge_count
        )
        if bucket == 0:
            target_half = gather_cols(table, target_ids[0])
        else:
            target_half = answered[bucket].astype(jnp.float32)
        target_rows = target_half.reshape(halves, columns, edge_count)
        product = jnp.stack(
            [
                source_rows[0] * relation_rows[0] - source_rows[1] * relation_rows[1],
                source_rows[0] * relation_rows[1] + source_rows[1] * relation_rows[0],
            ]
        )
        rounded = product.astype(jnp.bfloat16)
        rounded_wide = rounded.astype(jnp.float32)
        positive_part = jnp.sum(rounded_wide * target_rows, axis=(0, 1))
        negative_rows = gather_cols(pool_flat, negative_flat).astype(jnp.bfloat16).reshape(
            flat_width, spans, negs_per
        )
        query_rows = rounded.reshape(flat_width, spans, span_len)
        negative_part = lax.dot_general(
            query_rows,
            negative_rows,
            (((0,), (0,)), ((1,), (1,))),
            preferred_element_type=jnp.float32,
        ).reshape(spans, -1, 128)
        positive_rows = positive_part.reshape(spans, -1, 128)
        pad = jnp.zeros((spans, 16 - positive_rows.shape[1], 128), jnp.float32)
        partial = jnp.concatenate([negative_part, positive_rows, pad], axis=1).astype(
            jnp.bfloat16
        )
        state = (relation_rows, target_rows, rounded, rounded_wide, negative_rows, query_rows)
        return partial, state

    def gradients(bucket, reduced, state):
        relation_rows, target_rows, rounded, rounded_wide, negative_rows, query_rows = state
        negative_slope, positive_sums = reduced
        positive = positive_sums[:, : span_len // 128].reshape(edge_count)
        positive_slope = -jax.nn.sigmoid(-positive)
        slope_spans = negative_slope.reshape(spans, span_len, negs_per)
        pool_terms = lax.dot_general(
            query_rows,
            slope_spans,
            (((2,), (1,)), ((1,), (0,))),
            preferred_element_type=jnp.float32,
        ).transpose(1, 0, 2).reshape(flat_width, spans * negs_per)
        query_terms = lax.dot_general(
            slope_spans,
            negative_rows,
            (((2,), (2,)), ((0,), (1,))),
            preferred_element_type=jnp.float32,
        )
        query_terms = query_terms.transpose(2, 0, 1).reshape(halves, columns, edge_count)
        total_grad = positive_slope * target_rows + query_terms
        target_values = (positive_slope * rounded_wide).reshape(flat_width, edge_count)
        source_grad = jnp.stack(
            [
                total_grad[0] * relation_rows[0] + total_grad[1] * relation_rows[1],
                total_grad[1] * relation_rows[0] - total_grad[0] * relation_rows[1],
            ]
        ).reshape(flat_width, edge_count)
        return pool_terms, target_values, source_grad

    f32_values, f32_index = [], []
    pool_values, pool_index = [], []
    bf16_values, bf16_index = [], []
    results = [scores(bucket) for bucket in range(buckets)]
    negative_all, positive_all = col_exchange(jnp.stack([r[0] for r in results], axis=1))
    for done in range(buckets):
        reduced = (negative_all[:, done], positive_all[:, done])
        pool_terms, target_values, source_grad = gradients(done, reduced, results[done][1])
        pool_values.append(pool_terms)
        pool_index.append(negative_ids[done].reshape(-1))
        f32_values.append(source_grad)
        f32_index.append(source_ids[done])
        if done == 0:
            f32_values.append(target_values)
            f32_index.append(target_ids[0])
        else:
            bf16_values.append(shifted(target_values.astype(jnp.bfloat16), "dom", -done))
            bf16_index.append(asked[done])

    pool_grad = scatter_f32(
        jnp.concatenate(pool_values, axis=1), jnp.concatenate(pool_index), pool_count
    ).T
    returned = lax.all_to_all(
        pool_grad.reshape(halves, columns, -1).astype(jnp.bfloat16),
        "dom",
        split_axis=2,
        concat_axis=2,
        tiled=True,
    ).reshape(flat_width, -1)
    bf16_values.append(returned)
    bf16_index.append(served_flat)
    lane_width = 128
    high, low = split_exact(jnp.concatenate(f32_values, axis=1))
    wide = scatter_pallas(
        jnp.concatenate([padded_t(high, lane_width), padded_t(low, lane_width)], axis=1),
        jnp.concatenate(f32_index),
        entities,
    )
    narrow = scatter_pallas(
        padded_t(jnp.concatenate(bf16_values, axis=1), lane_width),
        jnp.concatenate(bf16_index),
        entities,
    )
    owned = (
        wide[:, :flat_width] + wide[:, lane_width:lane_width + flat_width] + narrow[:, :flat_width]
    )
    return owned.T.reshape(halves, columns, entities)


def solution(mesh):
    placed = (
        P(None, "col", "dom"),
        P(None, "col", None),
        P(None, "dom"),
        P(None, "dom"),
        P(None, "dom"),
        P(None, "dom", None),
        P("dom", None),
    )
    return jax.shard_map(
        body, mesh=mesh, in_specs=placed, out_specs=P(None, "col", "dom"), check_vma=False
    )
```

```python
import functools

import jax
import jax.numpy as jnp
from jax import lax
from jax.experimental import pallas as pl
from jax.experimental.pallas import tpu as pltpu
from jax.sharding import PartitionSpec as P

MESH_ID = pl.DeviceIdType.MESH


def exchange_kernel(batches, neg_rows, partial_ref, neg_out, pos_out,
                    received, crossing, arrived, slopes, sums,
                    send_a, recv_a, send_x, recv_x, send_b, recv_b, send_c, recv_c):
    me = lax.axis_index("col")
    dom = lax.axis_index("dom")
    pair = me + 1 - 2 * lax.rem(me, 2)
    cross = lax.rem(me + 2, 4)
    far = lax.rem(pair + 2, 4)

    barrier = pltpu.get_barrier_semaphore()
    for other in (pair, cross):
        pl.semaphore_signal(barrier, inc=1, device_id=(dom, other), device_id_type=MESH_ID)
    pl.semaphore_wait(barrier, 2)

    def on_chip(batch, slot, span):
        return pltpu.make_async_remote_copy(
            src_ref=partial_ref.at[span, batch], dst_ref=received.at[slot, batch],
            send_sem=send_a.at[batch * 2 + slot], recv_sem=recv_a.at[batch * 2 + slot],
            device_id=(dom, pair), device_id_type=MESH_ID)

    def across(batch):
        return pltpu.make_async_remote_copy(
            src_ref=crossing.at[batch], dst_ref=arrived.at[batch],
            send_sem=send_x.at[batch], recv_sem=recv_x.at[batch],
            device_id=(dom, cross), device_id_type=MESH_ID)

    def slope_copies(batch, span, dst, route):
        return (
            pltpu.make_async_remote_copy(
                src_ref=slopes.at[span, batch], dst_ref=slopes.at[span, batch],
                send_sem=send_b.at[batch * 3 + route], recv_sem=recv_b.at[batch * 4 + span],
                device_id=(dom, dst), device_id_type=MESH_ID),
            pltpu.make_async_remote_copy(
                src_ref=sums.at[span, batch], dst_ref=sums.at[span, batch],
                send_sem=send_c.at[batch * 3 + route], recv_sem=recv_c.at[batch * 4 + span],
                device_id=(dom, dst), device_id_type=MESH_ID),
        )

    started = []
    for batch in range(batches):
        for copy in (on_chip(batch, 0, pair), on_chip(batch, 1, far)):
            copy.start()
            started.append(copy)
    for batch in range(batches):
        on_chip(batch, 0, me).wait_recv()
        on_chip(batch, 1, cross).wait_recv()
        crossing[batch] = (
            partial_ref[cross, batch].astype(jnp.float32) + received[1, batch].astype(jnp.float32)
        ).astype(crossing.dtype)
        copy = across(batch)
        copy.start()
        started.append(copy)
    for batch in range(batches):
        across(batch).wait_recv()
        total = (
            partial_ref[me, batch].astype(jnp.float32)
            + received[0, batch].astype(jnp.float32)
            + arrived[batch].astype(jnp.float32)
        )
        slopes[me, batch] = (1.0 / (1.0 + jnp.exp(-total[:neg_rows]))).astype(slopes.dtype)
        sums[me, batch] = total[neg_rows:neg_rows + 8]
        for copy in slope_copies(batch, me, cross, 0) + slope_copies(batch, me, pair, 1):
            copy.start()
            started.append(copy)
    for batch in range(batches):
        for copy in slope_copies(batch, cross, me, 0):
            copy.wait_recv()
        for copy in slope_copies(batch, cross, pair, 2):
            copy.start()
            started.append(copy)
    for batch in range(batches):
        for copy in slope_copies(batch, pair, me, 1) + slope_copies(batch, far, me, 2):
            copy.wait_recv()
    for copy in started:
        copy.wait_send()
    neg_out[...] = slopes[...]
    pos_out[...] = sums[...]


def col_exchange(partial):
    parts, batches, rows, lanes = partial.shape
    neg_rows = rows - 16
    vmem = pl.BlockSpec(memory_space=pltpu.VMEM)
    return pl.pallas_call(
        functools.partial(exchange_kernel, batches, neg_rows),
        out_shape=(
            jax.ShapeDtypeStruct((parts, batches, neg_rows, lanes), jnp.bfloat16),
            jax.ShapeDtypeStruct((parts, batches, 8, lanes), jnp.float32),
        ),
        in_specs=[vmem],
        out_specs=(vmem, vmem),
        scratch_shapes=[
            pltpu.VMEM((2, batches, rows, lanes), jnp.bfloat16),
            pltpu.VMEM((batches, rows, lanes), jnp.bfloat16),
            pltpu.VMEM((batches, rows, lanes), jnp.bfloat16),
            pltpu.VMEM((parts, batches, neg_rows, lanes), jnp.bfloat16),
            pltpu.VMEM((parts, batches, 8, lanes), jnp.float32),
            pltpu.SemaphoreType.DMA((2 * batches,)),
            pltpu.SemaphoreType.DMA((2 * batches,)),
            pltpu.SemaphoreType.DMA((batches,)),
            pltpu.SemaphoreType.DMA((batches,)),
            pltpu.SemaphoreType.DMA((3 * batches,)),
            pltpu.SemaphoreType.DMA((parts * batches,)),
            pltpu.SemaphoreType.DMA((3 * batches,)),
            pltpu.SemaphoreType.DMA((parts * batches,)),
        ],
        compiler_params=pltpu.CompilerParams(
            collective_id=0, has_side_effects=True, vmem_limit_bytes=48 * 1024 * 1024
        ),
    )(partial)


def scatter_kernel(count, tile, chunk, ids_ref, values_ref, out_ref):
    width = ids_ref.shape[1]
    out_ref[...] = jnp.zeros_like(out_ref)
    column = lax.broadcasted_iota(jnp.int32, (tile, 1), 0)

    def per_tile(block, carry):
        first = pl.multiple_of(block * tile, tile)

        def per_chunk(step, inner):
            start = pl.multiple_of(step * chunk, chunk)
            offsets = ids_ref[:, pl.ds(start, chunk)] - first
            one_hot = jnp.where(column == offsets, 1.0, 0.0).astype(values_ref.dtype)
            out_ref[pl.ds(first, tile), :] += jnp.dot(
                one_hot, values_ref[pl.ds(start, chunk), :], preferred_element_type=jnp.float32
            )
            return inner

        return lax.fori_loop(0, width // chunk, per_chunk, carry)

    lax.fori_loop(0, count // tile, per_tile, 0)


def scatter_pallas(values_t, indices, count):
    tile, chunk = 1024, 1024
    vmem = pl.BlockSpec(memory_space=pltpu.VMEM)
    return pl.pallas_call(
        functools.partial(scatter_kernel, count, tile, chunk),
        out_shape=jax.ShapeDtypeStruct((count, values_t.shape[1]), jnp.float32),
        in_specs=[vmem, vmem],
        out_specs=vmem,
        compiler_params=pltpu.CompilerParams(vmem_limit_bytes=48 * 1024 * 1024),
    )(indices.reshape(1, -1), values_t)


def padded_t(values, width):
    rows = values.shape[0]
    return jnp.pad(values, ((0, width - rows), (0, 0))).T


def shifted(shard, axis, by):
    size = lax.axis_size(axis)
    return lax.ppermute(shard, axis, [(i, (i + by) % size) for i in range(size)])


def gather_cols(table, indices):
    count = table.shape[1]
    one_hot = (
        lax.broadcasted_iota(jnp.int32, (count, indices.shape[0]), 0) == indices[None, :]
    ).astype(table.dtype)
    return jnp.dot(table, one_hot, preferred_element_type=jnp.float32)


def split_exact(values):
    high = values.astype(jnp.bfloat16)
    low = (values - high.astype(jnp.float32)).astype(jnp.bfloat16)
    return high, low


def scatter_rows(values, indices, count):
    one_hot = (
        lax.broadcasted_iota(jnp.int32, (count, indices.shape[0]), 0) == indices[None, :]
    ).astype(jnp.bfloat16)
    return lax.dot_general(
        one_hot, values, (((1,), (1,)), ((), ())), preferred_element_type=jnp.float32
    )


def scatter_f32(values, indices, count):
    rows = values.shape[0]
    high, low = split_exact(values)
    summed = scatter_rows(jnp.concatenate([high, low], axis=0), indices, count)
    return summed[:, :rows] + summed[:, rows:]


def body(embeddings, relations, source_ids, relation_ids, target_ids, negative_ids, served_rows):
    halves, columns, entities = embeddings.shape
    flat_width = halves * columns
    buckets, edge_count = source_ids.shape
    spans, negs_per = (negative_ids.shape[1], negative_ids.shape[2])
    span_len = edge_count // spans
    table = embeddings.reshape(flat_width, entities)
    relation_flat = relations.reshape(flat_width, relations.shape[2])
    served_flat = served_rows.reshape(-1)

    asked = [None] + [shifted(target_ids[b], "dom", -b) for b in range(1, buckets)]
    answered = [None] + [
        shifted(gather_cols(table, asked[b]).astype(jnp.bfloat16), "dom", b)
        for b in range(1, buckets)
    ]

    fetched = gather_cols(table, served_flat).astype(jnp.bfloat16)
    negative_pool = lax.all_to_all(
        fetched.reshape(halves, columns, -1), "dom", split_axis=2, concat_axis=2, tiled=True
    )
    pool_flat = negative_pool.reshape(flat_width, -1)
    pool_count = pool_flat.shape[1]

    def scores(bucket):
        negative_flat = negative_ids[bucket].reshape(-1)
        source_rows = gather_cols(table, source_ids[bucket]).reshape(halves, columns, edge_count)
        relation_rows = gather_cols(relation_flat, relation_ids[bucket]).reshape(
            halves, columns, edge_count
        )
        if bucket == 0:
            target_half = gather_cols(table, target_ids[0])
        else:
            target_half = answered[bucket].astype(jnp.float32)
        target_rows = target_half.reshape(halves, columns, edge_count)
        product = jnp.stack(
            [
                source_rows[0] * relation_rows[0] - source_rows[1] * relation_rows[1],
                source_rows[0] * relation_rows[1] + source_rows[1] * relation_rows[0],
            ]
        )
        rounded = product.astype(jnp.bfloat16)
        rounded_wide = rounded.astype(jnp.float32)
        positive_part = jnp.sum(rounded_wide * target_rows, axis=(0, 1))
        negative_rows = gather_cols(pool_flat, negative_flat).astype(jnp.bfloat16).reshape(
            flat_width, spans, negs_per
        )
        query_rows = rounded.reshape(flat_width, spans, span_len)
        negative_part = lax.dot_general(
            query_rows,
            negative_rows,
            (((0,), (0,)), ((1,), (1,))),
            preferred_element_type=jnp.float32,
        ).reshape(spans, -1, 128)
        positive_rows = positive_part.reshape(spans, -1, 128)
        pad = jnp.zeros((spans, 16 - positive_rows.shape[1], 128), jnp.float32)
        partial = jnp.concatenate([negative_part, positive_rows, pad], axis=1).astype(
            jnp.bfloat16
        )
        state = (relation_rows, target_rows, rounded, rounded_wide, negative_rows, query_rows)
        return partial, state

    def gradients(bucket, reduced, state):
        relation_rows, target_rows, rounded, rounded_wide, negative_rows, query_rows = state
        negative_slope, positive_sums = reduced
        positive = positive_sums[:, : span_len // 128].reshape(edge_count)
        positive_slope = -jax.nn.sigmoid(-positive)
        slope_spans = negative_slope.reshape(spans, span_len, negs_per)
        pool_terms = lax.dot_general(
            query_rows,
            slope_spans,
            (((2,), (1,)), ((1,), (0,))),
            preferred_element_type=jnp.float32,
        ).transpose(1, 0, 2).reshape(flat_width, spans * negs_per)
        query_terms = lax.dot_general(
            slope_spans,
            negative_rows,
            (((2,), (2,)), ((0,), (1,))),
            preferred_element_type=jnp.float32,
        )
        query_terms = query_terms.transpose(2, 0, 1).reshape(halves, columns, edge_count)
        total_grad = positive_slope * target_rows + query_terms
        target_values = (positive_slope * rounded_wide).reshape(flat_width, edge_count)
        source_grad = jnp.stack(
            [
                total_grad[0] * relation_rows[0] + total_grad[1] * relation_rows[1],
                total_grad[1] * relation_rows[0] - total_grad[0] * relation_rows[1],
            ]
        ).reshape(flat_width, edge_count)
        return pool_terms, target_values, source_grad

    f32_values, f32_index = [], []
    pool_values, pool_index = [], []
    bf16_values, bf16_index = [], []
    results = [scores(bucket) for bucket in range(buckets)]
    negative_all, positive_all = col_exchange(jnp.stack([r[0] for r in results], axis=1))
    for done in range(buckets):
        reduced = (negative_all[:, done], positive_all[:, done])
        pool_terms, target_values, source_grad = gradients(done, reduced, results[done][1])
        pool_values.append(pool_terms)
        pool_index.append(negative_ids[done].reshape(-1))
        f32_values.append(source_grad)
        f32_index.append(source_ids[done])
        if done == 0:
            f32_values.append(target_values)
            f32_index.append(target_ids[0])
        else:
            bf16_values.append(shifted(target_values.astype(jnp.bfloat16), "dom", -done))
            bf16_index.append(asked[done])

    pool_grad = scatter_f32(
        jnp.concatenate(pool_values, axis=1), jnp.concatenate(pool_index), pool_count
    ).T
    returned = lax.all_to_all(
        pool_grad.reshape(halves, columns, -1).astype(jnp.bfloat16),
        "dom",
        split_axis=2,
        concat_axis=2,
        tiled=True,
    ).reshape(flat_width, -1)
    bf16_values.append(returned)
    bf16_index.append(served_flat)
    lane_width = 128
    high, low = split_exact(jnp.concatenate(f32_values, axis=1))
    wide = scatter_pallas(
        jnp.concatenate([padded_t(high, lane_width), padded_t(low, lane_width)], axis=1),
        jnp.concatenate(f32_index),
        entities,
    )
    narrow = scatter_pallas(
        padded_t(jnp.concatenate(bf16_values, axis=1), lane_width),
        jnp.concatenate(bf16_index),
        entities,
    )
    owned = (
        wide[:, :flat_width] + wide[:, lane_width:lane_width + flat_width] + narrow[:, :flat_width]
    )
    return owned.T.reshape(halves, columns, entities)


def solution(mesh):
    placed = (
        P(None, "col", "dom"),
        P(None, "col", None),
        P(None, "dom"),
        P(None, "dom"),
        P(None, "dom"),
        P(None, "dom", None),
        P("dom", None),
    )
    return jax.shard_map(
        body, mesh=mesh, in_specs=placed, out_specs=P(None, "col", "dom"), check_vma=False
    )
```

```python
import functools

import jax
import jax.numpy as jnp
from jax import lax
from jax.experimental import pallas as pl
from jax.experimental.pallas import tpu as pltpu
from jax.sharding import PartitionSpec as P

MESH_ID = pl.DeviceIdType.MESH


def exchange_kernel(batches, neg_rows, partial_ref, neg_out, pos_out,
                    received, crossing, arrived, slopes, sums,
                    send_a, recv_a, send_x, recv_x, send_b, recv_b, send_c, recv_c):
    me = lax.axis_index("col")
    dom = lax.axis_index("dom")
    pair = me + 1 - 2 * lax.rem(me, 2)
    cross = lax.rem(me + 2, 4)
    far = lax.rem(pair + 2, 4)

    barrier = pltpu.get_barrier_semaphore()
    for other in (pair, cross):
        pl.semaphore_signal(barrier, inc=1, device_id=(dom, other), device_id_type=MESH_ID)
    pl.semaphore_wait(barrier, 2)

    def on_chip(batch, slot, span):
        return pltpu.make_async_remote_copy(
            src_ref=partial_ref.at[span, batch], dst_ref=received.at[slot, batch],
            send_sem=send_a.at[batch * 2 + slot], recv_sem=recv_a.at[batch * 2 + slot],
            device_id=(dom, pair), device_id_type=MESH_ID)

    def across(batch):
        return pltpu.make_async_remote_copy(
            src_ref=crossing.at[batch], dst_ref=arrived.at[batch],
            send_sem=send_x.at[batch], recv_sem=recv_x.at[batch],
            device_id=(dom, cross), device_id_type=MESH_ID)

    def slope_copies(batch, span, dst, route):
        return (
            pltpu.make_async_remote_copy(
                src_ref=slopes.at[span, batch], dst_ref=slopes.at[span, batch],
                send_sem=send_b.at[batch * 3 + route], recv_sem=recv_b.at[batch * 4 + span],
                device_id=(dom, dst), device_id_type=MESH_ID),
            pltpu.make_async_remote_copy(
                src_ref=sums.at[span, batch], dst_ref=sums.at[span, batch],
                send_sem=send_c.at[batch * 3 + route], recv_sem=recv_c.at[batch * 4 + span],
                device_id=(dom, dst), device_id_type=MESH_ID),
        )

    started = []
    for batch in range(batches):
        for copy in (on_chip(batch, 0, pair), on_chip(batch, 1, far)):
            copy.start()
            started.append(copy)
    for batch in range(batches):
        on_chip(batch, 0, me).wait_recv()
        on_chip(batch, 1, cross).wait_recv()
        crossing[batch] = (
            partial_ref[cross, batch].astype(jnp.float32) + received[1, batch].astype(jnp.float32)
        ).astype(crossing.dtype)
        copy = across(batch)
        copy.start()
        started.append(copy)
    for batch in range(batches):
        across(batch).wait_recv()
        total = (
            partial_ref[me, batch].astype(jnp.float32)
            + received[0, batch].astype(jnp.float32)
            + arrived[batch].astype(jnp.float32)
        )
        slopes[me, batch] = (1.0 / (1.0 + jnp.exp(-total[:neg_rows]))).astype(slopes.dtype)
        sums[me, batch] = total[neg_rows:neg_rows + 8]
        for copy in slope_copies(batch, me, cross, 0) + slope_copies(batch, me, pair, 1):
            copy.start()
            started.append(copy)
    for batch in range(batches):
        for copy in slope_copies(batch, cross, me, 0):
            copy.wait_recv()
        for copy in slope_copies(batch, cross, pair, 2):
            copy.start()
            started.append(copy)
    for batch in range(batches):
        for copy in slope_copies(batch, pair, me, 1) + slope_copies(batch, far, me, 2):
            copy.wait_recv()
    for copy in started:
        copy.wait_send()
    neg_out[...] = slopes[...]
    pos_out[...] = sums[...]


def col_exchange(partial):
    parts, batches, rows, lanes = partial.shape
    neg_rows = rows - 16
    vmem = pl.BlockSpec(memory_space=pltpu.VMEM)
    return pl.pallas_call(
        functools.partial(exchange_kernel, batches, neg_rows),
        out_shape=(
            jax.ShapeDtypeStruct((parts, batches, neg_rows, lanes), jnp.bfloat16),
            jax.ShapeDtypeStruct((parts, batches, 8, lanes), jnp.float32),
        ),
        in_specs=[vmem],
        out_specs=(vmem, vmem),
        scratch_shapes=[
            pltpu.VMEM((2, batches, rows, lanes), jnp.bfloat16),
            pltpu.VMEM((batches, rows, lanes), jnp.bfloat16),
            pltpu.VMEM((batches, rows, lanes), jnp.bfloat16),
            pltpu.VMEM((parts, batches, neg_rows, lanes), jnp.bfloat16),
            pltpu.VMEM((parts, batches, 8, lanes), jnp.float32),
            pltpu.SemaphoreType.DMA((2 * batches,)),
            pltpu.SemaphoreType.DMA((2 * batches,)),
            pltpu.SemaphoreType.DMA((batches,)),
            pltpu.SemaphoreType.DMA((batches,)),
            pltpu.SemaphoreType.DMA((3 * batches,)),
            pltpu.SemaphoreType.DMA((parts * batches,)),
            pltpu.SemaphoreType.DMA((3 * batches,)),
            pltpu.SemaphoreType.DMA((parts * batches,)),
        ],
        compiler_params=pltpu.CompilerParams(
            collective_id=0, has_side_effects=True, vmem_limit_bytes=48 * 1024 * 1024
        ),
    )(partial)


def scatter_kernel(count, tile, chunk, ids_ref, values_ref, out_ref):
    width = ids_ref.shape[1]
    out_ref[...] = jnp.zeros_like(out_ref)
    column = lax.broadcasted_iota(jnp.int32, (tile, 1), 0)

    def per_tile(block, carry):
        first = pl.multiple_of(block * tile, tile)

        def per_chunk(step, inner):
            start = pl.multiple_of(step * chunk, chunk)
            offsets = ids_ref[:, pl.ds(start, chunk)] - first
            one_hot = jnp.where(column == offsets, 1.0, 0.0).astype(values_ref.dtype)
            out_ref[pl.ds(first, tile), :] += jnp.dot(
                one_hot, values_ref[pl.ds(start, chunk), :], preferred_element_type=jnp.float32
            )
            return inner

        return lax.fori_loop(0, width // chunk, per_chunk, carry)

    lax.fori_loop(0, count // tile, per_tile, 0)


def scatter_pallas(values_t, indices, count):
    tile, chunk = 1024, 1024
    vmem = pl.BlockSpec(memory_space=pltpu.VMEM)
    return pl.pallas_call(
        functools.partial(scatter_kernel, count, tile, chunk),
        out_shape=jax.ShapeDtypeStruct((count, values_t.shape[1]), jnp.float32),
        in_specs=[vmem, vmem],
        out_specs=vmem,
        compiler_params=pltpu.CompilerParams(vmem_limit_bytes=48 * 1024 * 1024),
        cost_estimate=pl.CostEstimate(
            flops=2 * count * values_t.shape[0] * values_t.shape[1],
            bytes_accessed=values_t.size * 2 + count * values_t.shape[1] * 4,
            transcendentals=0,
        ),
    )(indices.reshape(1, -1), values_t)


def padded_t(values, width):
    rows = values.shape[0]
    return jnp.pad(values, ((0, width - rows), (0, 0))).T


def shifted(shard, axis, by):
    size = lax.axis_size(axis)
    return lax.ppermute(shard, axis, [(i, (i + by) % size) for i in range(size)])


def gather_cols(table, indices):
    count = table.shape[1]
    one_hot = (
        lax.broadcasted_iota(jnp.int32, (count, indices.shape[0]), 0) == indices[None, :]
    ).astype(table.dtype)
    return jnp.dot(table, one_hot, preferred_element_type=jnp.float32)


def split_exact(values):
    high = values.astype(jnp.bfloat16)
    low = (values - high.astype(jnp.float32)).astype(jnp.bfloat16)
    return high, low


def scatter_rows(values, indices, count):
    one_hot = (
        lax.broadcasted_iota(jnp.int32, (count, indices.shape[0]), 0) == indices[None, :]
    ).astype(jnp.bfloat16)
    return lax.dot_general(
        one_hot, values, (((1,), (1,)), ((), ())), preferred_element_type=jnp.float32
    )


def scatter_f32(values, indices, count):
    rows = values.shape[0]
    high, low = split_exact(values)
    summed = scatter_rows(jnp.concatenate([high, low], axis=0), indices, count)
    return summed[:, :rows] + summed[:, rows:]


def body(embeddings, relations, source_ids, relation_ids, target_ids, negative_ids, served_rows):
    halves, columns, entities = embeddings.shape
    flat_width = halves * columns
    buckets, edge_count = source_ids.shape
    spans, negs_per = (negative_ids.shape[1], negative_ids.shape[2])
    span_len = edge_count // spans
    table = embeddings.reshape(flat_width, entities)
    relation_flat = relations.reshape(flat_width, relations.shape[2])
    served_flat = served_rows.reshape(-1)

    asked = [None] + [shifted(target_ids[b], "dom", -b) for b in range(1, buckets)]
    answered = [None] + [
        shifted(gather_cols(table, asked[b]).astype(jnp.bfloat16), "dom", b)
        for b in range(1, buckets)
    ]

    fetched = gather_cols(table, served_flat).astype(jnp.bfloat16)
    negative_pool = lax.all_to_all(
        fetched.reshape(halves, columns, -1), "dom", split_axis=2, concat_axis=2, tiled=True
    )
    pool_flat = negative_pool.reshape(flat_width, -1)
    pool_count = pool_flat.shape[1]

    def scores(bucket):
        negative_flat = negative_ids[bucket].reshape(-1)
        source_rows = gather_cols(table, source_ids[bucket]).reshape(halves, columns, edge_count)
        relation_rows = gather_cols(relation_flat, relation_ids[bucket]).reshape(
            halves, columns, edge_count
        )
        if bucket == 0:
            target_half = gather_cols(table, target_ids[0])
        else:
            target_half = answered[bucket].astype(jnp.float32)
        target_rows = target_half.reshape(halves, columns, edge_count)
        product = jnp.stack(
            [
                source_rows[0] * relation_rows[0] - source_rows[1] * relation_rows[1],
                source_rows[0] * relation_rows[1] + source_rows[1] * relation_rows[0],
            ]
        )
        rounded = product.astype(jnp.bfloat16)
        rounded_wide = rounded.astype(jnp.float32)
        positive_part = jnp.sum(rounded_wide * target_rows, axis=(0, 1))
        negative_rows = gather_cols(pool_flat, negative_flat).astype(jnp.bfloat16).reshape(
            flat_width, spans, negs_per
        )
        query_rows = rounded.reshape(flat_width, spans, span_len)
        negative_part = lax.dot_general(
            query_rows,
            negative_rows,
            (((0,), (0,)), ((1,), (1,))),
            preferred_element_type=jnp.float32,
        ).reshape(spans, -1, 128)
        positive_rows = positive_part.reshape(spans, -1, 128)
        pad = jnp.zeros((spans, 16 - positive_rows.shape[1], 128), jnp.float32)
        partial = jnp.concatenate([negative_part, positive_rows, pad], axis=1).astype(
            jnp.bfloat16
        )
        state = (relation_rows, target_rows, rounded, rounded_wide, negative_rows, query_rows)
        return partial, state

    def gradients(bucket, reduced, state):
        relation_rows, target_rows, rounded, rounded_wide, negative_rows, query_rows = state
        negative_slope, positive_sums = reduced
        positive = positive_sums[:, : span_len // 128].reshape(edge_count)
        positive_slope = -jax.nn.sigmoid(-positive)
        slope_spans = negative_slope.reshape(spans, span_len, negs_per)
        pool_terms = lax.dot_general(
            query_rows,
            slope_spans,
            (((2,), (1,)), ((1,), (0,))),
            preferred_element_type=jnp.float32,
        ).transpose(1, 0, 2).reshape(flat_width, spans * negs_per)
        query_terms = lax.dot_general(
            slope_spans,
            negative_rows,
            (((2,), (2,)), ((0,), (1,))),
            preferred_element_type=jnp.float32,
        )
        query_terms = query_terms.transpose(2, 0, 1).reshape(halves, columns, edge_count)
        total_grad = positive_slope * target_rows + query_terms
        target_values = (positive_slope * rounded_wide).reshape(flat_width, edge_count)
        source_grad = jnp.stack(
            [
                total_grad[0] * relation_rows[0] + total_grad[1] * relation_rows[1],
                total_grad[1] * relation_rows[0] - total_grad[0] * relation_rows[1],
            ]
        ).reshape(flat_width, edge_count)
        return pool_terms, target_values, source_grad

    f32_values, f32_index = [], []
    pool_values, pool_index = [], []
    bf16_values, bf16_index = [], []
    results = [scores(bucket) for bucket in range(buckets)]
    negative_all, positive_all = col_exchange(jnp.stack([r[0] for r in results], axis=1))
    for done in range(buckets):
        reduced = (negative_all[:, done], positive_all[:, done])
        pool_terms, target_values, source_grad = gradients(done, reduced, results[done][1])
        pool_values.append(pool_terms)
        pool_index.append(negative_ids[done].reshape(-1))
        f32_values.append(source_grad)
        f32_index.append(source_ids[done])
        if done == 0:
            f32_values.append(target_values)
            f32_index.append(target_ids[0])
        else:
            bf16_values.append(shifted(target_values.astype(jnp.bfloat16), "dom", -done))
            bf16_index.append(asked[done])

    pool_grad = scatter_f32(
        jnp.concatenate(pool_values, axis=1), jnp.concatenate(pool_index), pool_count
    ).T
    returned = lax.all_to_all(
        pool_grad.reshape(halves, columns, -1).astype(jnp.bfloat16),
        "dom",
        split_axis=2,
        concat_axis=2,
        tiled=True,
    ).reshape(flat_width, -1)
    bf16_values.append(returned)
    bf16_index.append(served_flat)
    lane_width = 128
    high, low = split_exact(jnp.concatenate(f32_values, axis=1))
    wide = scatter_pallas(
        jnp.concatenate([padded_t(high, lane_width), padded_t(low, lane_width)], axis=1),
        jnp.concatenate(f32_index),
        entities,
    )
    narrow = scatter_pallas(
        padded_t(jnp.concatenate(bf16_values, axis=1), lane_width),
        jnp.concatenate(bf16_index),
        entities,
    )
    owned = (
        wide[:, :flat_width] + wide[:, lane_width:lane_width + flat_width] + narrow[:, :flat_width]
    )
    return owned.T.reshape(halves, columns, entities)


def solution(mesh):
    placed = (
        P(None, "col", "dom"),
        P(None, "col", None),
        P(None, "dom"),
        P(None, "dom"),
        P(None, "dom"),
        P(None, "dom", None),
        P("dom", None),
    )
    return jax.shard_map(
        body, mesh=mesh, in_specs=placed, out_specs=P(None, "col", "dom"), check_vma=False
    )
```

```python
import functools

import jax
import jax.numpy as jnp
from jax import lax
from jax.experimental import pallas as pl
from jax.experimental.pallas import tpu as pltpu
from jax.sharding import PartitionSpec as P

MESH_ID = pl.DeviceIdType.MESH


def exchange_kernel(batches, neg_rows, partial_ref, neg_out, pos_out,
                    received, crossing, arrived, slopes, sums,
                    send_a, recv_a, send_x, recv_x, send_b, recv_b, send_c, recv_c):
    me = lax.axis_index("col")
    dom = lax.axis_index("dom")
    pair = me + 1 - 2 * lax.rem(me, 2)
    cross = lax.rem(me + 2, 4)
    far = lax.rem(pair + 2, 4)

    barrier = pltpu.get_barrier_semaphore()
    for other in (pair, cross):
        pl.semaphore_signal(barrier, inc=1, device_id=(dom, other), device_id_type=MESH_ID)
    pl.semaphore_wait(barrier, 2)

    def on_chip(batch, slot, span):
        return pltpu.make_async_remote_copy(
            src_ref=partial_ref.at[span, batch], dst_ref=received.at[slot, batch],
            send_sem=send_a.at[batch * 2 + slot], recv_sem=recv_a.at[batch * 2 + slot],
            device_id=(dom, pair), device_id_type=MESH_ID)

    def across(batch):
        return pltpu.make_async_remote_copy(
            src_ref=crossing.at[batch], dst_ref=arrived.at[batch],
            send_sem=send_x.at[batch], recv_sem=recv_x.at[batch],
            device_id=(dom, cross), device_id_type=MESH_ID)

    def slope_copies(batch, span, dst, route):
        return (
            pltpu.make_async_remote_copy(
                src_ref=slopes.at[span, batch], dst_ref=slopes.at[span, batch],
                send_sem=send_b.at[batch * 3 + route], recv_sem=recv_b.at[batch * 4 + span],
                device_id=(dom, dst), device_id_type=MESH_ID),
            pltpu.make_async_remote_copy(
                src_ref=sums.at[span, batch], dst_ref=sums.at[span, batch],
                send_sem=send_c.at[batch * 3 + route], recv_sem=recv_c.at[batch * 4 + span],
                device_id=(dom, dst), device_id_type=MESH_ID),
        )

    started = []
    for batch in range(batches):
        for copy in (on_chip(batch, 0, pair), on_chip(batch, 1, far)):
            copy.start()
            started.append(copy)
    for batch in range(batches):
        on_chip(batch, 0, me).wait_recv()
        on_chip(batch, 1, cross).wait_recv()
        crossing[batch] = (
            partial_ref[cross, batch].astype(jnp.float32) + received[1, batch].astype(jnp.float32)
        ).astype(crossing.dtype)
        copy = across(batch)
        copy.start()
        started.append(copy)
    for batch in range(batches):
        across(batch).wait_recv()
        total = (
            partial_ref[me, batch].astype(jnp.float32)
            + received[0, batch].astype(jnp.float32)
            + arrived[batch].astype(jnp.float32)
        )
        slopes[me, batch] = (1.0 / (1.0 + jnp.exp(-total[:neg_rows]))).astype(slopes.dtype)
        sums[me, batch] = total[neg_rows:neg_rows + 8]
        for copy in slope_copies(batch, me, cross, 0) + slope_copies(batch, me, pair, 1):
            copy.start()
            started.append(copy)
    for batch in range(batches):
        for copy in slope_copies(batch, cross, me, 0):
            copy.wait_recv()
        for copy in slope_copies(batch, cross, pair, 2):
            copy.start()
            started.append(copy)
    for batch in range(batches):
        for copy in slope_copies(batch, pair, me, 1) + slope_copies(batch, far, me, 2):
            copy.wait_recv()
    for copy in started:
        copy.wait_send()
    neg_out[...] = slopes[...]
    pos_out[...] = sums[...]


def col_exchange(partial):
    parts, batches, rows, lanes = partial.shape
    neg_rows = rows - 16
    vmem = pl.BlockSpec(memory_space=pltpu.VMEM)
    return pl.pallas_call(
        functools.partial(exchange_kernel, batches, neg_rows),
        out_shape=(
            jax.ShapeDtypeStruct((parts, batches, neg_rows, lanes), jnp.bfloat16),
            jax.ShapeDtypeStruct((parts, batches, 8, lanes), jnp.float32),
        ),
        in_specs=[vmem],
        out_specs=(vmem, vmem),
        scratch_shapes=[
            pltpu.VMEM((2, batches, rows, lanes), jnp.bfloat16),
            pltpu.VMEM((batches, rows, lanes), jnp.bfloat16),
            pltpu.VMEM((batches, rows, lanes), jnp.bfloat16),
            pltpu.VMEM((parts, batches, neg_rows, lanes), jnp.bfloat16),
            pltpu.VMEM((parts, batches, 8, lanes), jnp.float32),
            pltpu.SemaphoreType.DMA((2 * batches,)),
            pltpu.SemaphoreType.DMA((2 * batches,)),
            pltpu.SemaphoreType.DMA((batches,)),
            pltpu.SemaphoreType.DMA((batches,)),
            pltpu.SemaphoreType.DMA((3 * batches,)),
            pltpu.SemaphoreType.DMA((parts * batches,)),
            pltpu.SemaphoreType.DMA((3 * batches,)),
            pltpu.SemaphoreType.DMA((parts * batches,)),
        ],
        compiler_params=pltpu.CompilerParams(
            collective_id=0, has_side_effects=True, vmem_limit_bytes=48 * 1024 * 1024
        ),
    )(partial)


def shifted(shard, axis, by):
    size = lax.axis_size(axis)
    return lax.ppermute(shard, axis, [(i, (i + by) % size) for i in range(size)])


def gather_cols(table, indices):
    count = table.shape[1]
    one_hot = (
        lax.broadcasted_iota(jnp.int32, (count, indices.shape[0]), 0) == indices[None, :]
    ).astype(table.dtype)
    return jnp.dot(table, one_hot, preferred_element_type=jnp.float32)


def split_exact(values):
    high = values.astype(jnp.bfloat16)
    low = (values - high.astype(jnp.float32)).astype(jnp.bfloat16)
    return high, low


def scatter_rows(values, indices, count):
    one_hot = (
        lax.broadcasted_iota(jnp.int32, (count, indices.shape[0]), 0) == indices[None, :]
    ).astype(jnp.bfloat16)
    return lax.dot_general(
        one_hot, values, (((1,), (1,)), ((), ())), preferred_element_type=jnp.float32
    )


def scatter_f32(values, indices, count):
    rows = values.shape[0]
    high, low = split_exact(values)
    summed = scatter_rows(jnp.concatenate([high, low], axis=0), indices, count)
    return summed[:, :rows] + summed[:, rows:]


def body(embeddings, relations, source_ids, relation_ids, target_ids, negative_ids, served_rows):
    halves, columns, entities = embeddings.shape
    flat_width = halves * columns
    buckets, edge_count = source_ids.shape
    spans, negs_per = (negative_ids.shape[1], negative_ids.shape[2])
    span_len = edge_count // spans
    table = embeddings.reshape(flat_width, entities)
    relation_flat = relations.reshape(flat_width, relations.shape[2])
    served_flat = served_rows.reshape(-1)

    asked = [None] + [shifted(target_ids[b], "dom", -b) for b in range(1, buckets)]
    fetched = gather_cols(table, served_flat).astype(jnp.bfloat16)
    serving = [gather_cols(table, asked[b]).astype(jnp.bfloat16) for b in range(1, buckets)]
    table, *serving = lax.optimization_barrier((table, *serving))
    answered = [None] + [shifted(serving[b - 1], "dom", b) for b in range(1, buckets)]

    negative_pool = lax.all_to_all(
        fetched.reshape(halves, columns, -1), "dom", split_axis=2, concat_axis=2, tiled=True
    )
    pool_flat = negative_pool.reshape(flat_width, -1)
    pool_count = pool_flat.shape[1]

    def scores(bucket):
        negative_flat = negative_ids[bucket].reshape(-1)
        source_rows = gather_cols(table, source_ids[bucket]).reshape(halves, columns, edge_count)
        relation_rows = gather_cols(relation_flat, relation_ids[bucket]).reshape(
            halves, columns, edge_count
        )
        if bucket == 0:
            target_half = gather_cols(table, target_ids[0])
        else:
            target_half = answered[bucket].astype(jnp.float32)
        target_rows = target_half.reshape(halves, columns, edge_count)
        product = jnp.stack(
            [
                source_rows[0] * relation_rows[0] - source_rows[1] * relation_rows[1],
                source_rows[0] * relation_rows[1] + source_rows[1] * relation_rows[0],
            ]
        )
        rounded = product.astype(jnp.bfloat16)
        rounded_wide = rounded.astype(jnp.float32)
        positive_part = jnp.sum(rounded_wide * target_rows, axis=(0, 1))
        negative_rows = gather_cols(pool_flat, negative_flat).astype(jnp.bfloat16).reshape(
            flat_width, spans, negs_per
        )
        query_rows = rounded.reshape(flat_width, spans, span_len)
        negative_part = lax.dot_general(
            query_rows,
            negative_rows,
            (((0,), (0,)), ((1,), (1,))),
            preferred_element_type=jnp.float32,
        ).reshape(spans, -1, 128)
        positive_rows = positive_part.reshape(spans, -1, 128)
        pad = jnp.zeros((spans, 16 - positive_rows.shape[1], 128), jnp.float32)
        partial = jnp.concatenate([negative_part, positive_rows, pad], axis=1).astype(
            jnp.bfloat16
        )
        state = (relation_rows, target_rows, rounded, rounded_wide, negative_rows, query_rows)
        return partial, state

    def gradients(bucket, reduced, state):
        relation_rows, target_rows, rounded, rounded_wide, negative_rows, query_rows = state
        negative_slope, positive_sums = reduced
        positive = positive_sums[:, : span_len // 128].reshape(edge_count)
        positive_slope = -jax.nn.sigmoid(-positive)
        slope_spans = negative_slope.reshape(spans, span_len, negs_per)
        pool_terms = lax.dot_general(
            query_rows,
            slope_spans,
            (((2,), (1,)), ((1,), (0,))),
            preferred_element_type=jnp.float32,
        ).transpose(1, 0, 2).reshape(flat_width, spans * negs_per)
        query_terms = lax.dot_general(
            slope_spans,
            negative_rows,
            (((2,), (2,)), ((0,), (1,))),
            preferred_element_type=jnp.float32,
        )
        query_terms = query_terms.transpose(2, 0, 1).reshape(halves, columns, edge_count)
        total_grad = positive_slope * target_rows + query_terms
        target_values = (positive_slope * rounded_wide).reshape(flat_width, edge_count)
        source_grad = jnp.stack(
            [
                total_grad[0] * relation_rows[0] + total_grad[1] * relation_rows[1],
                total_grad[1] * relation_rows[0] - total_grad[0] * relation_rows[1],
            ]
        ).reshape(flat_width, edge_count)
        return pool_terms, target_values, source_grad

    owned = jnp.zeros((entities, flat_width), jnp.float32)
    pool_values, pool_index = [], []
    bf16_values, bf16_index = [], []
    results = [scores(bucket) for bucket in range(buckets)]
    negative_all, positive_all = col_exchange(jnp.stack([r[0] for r in results], axis=1))
    for done in range(buckets):
        reduced = (negative_all[:, done], positive_all[:, done])
        pool_terms, target_values, source_grad = gradients(done, reduced, results[done][1])
        pool_values.append(pool_terms)
        pool_index.append(negative_ids[done].reshape(-1))
        if done == 0:
            owned = owned + scatter_f32(
                jnp.concatenate([source_grad, target_values], axis=1),
                jnp.concatenate([source_ids[0], target_ids[0]]),
                entities,
            )
        else:
            owned = owned + scatter_f32(source_grad, source_ids[done], entities)
            bf16_values.append(shifted(target_values.astype(jnp.bfloat16), "dom", -done))
            bf16_index.append(asked[done])

    pool_grad = scatter_f32(
        jnp.concatenate(pool_values, axis=1), jnp.concatenate(pool_index), pool_count
    ).T
    returned = lax.all_to_all(
        pool_grad.reshape(halves, columns, -1).astype(jnp.bfloat16),
        "dom",
        split_axis=2,
        concat_axis=2,
        tiled=True,
    ).reshape(flat_width, -1)
    bf16_values.append(returned)
    bf16_index.append(served_flat)
    owned = owned + scatter_rows(
        jnp.concatenate(bf16_values, axis=1), jnp.concatenate(bf16_index), entities
    )
    return owned.T.reshape(halves, columns, entities)


def solution(mesh):
    placed = (
        P(None, "col", "dom"),
        P(None, "col", None),
        P(None, "dom"),
        P(None, "dom"),
        P(None, "dom"),
        P(None, "dom", None),
        P("dom", None),
    )
    return jax.shard_map(
        body, mesh=mesh, in_specs=placed, out_specs=P(None, "col", "dom"), check_vma=False
    )
```

```python
import functools

import jax
import jax.numpy as jnp
from jax import lax
from jax.experimental import pallas as pl
from jax.experimental.pallas import tpu as pltpu
from jax.sharding import PartitionSpec as P

MESH_ID = pl.DeviceIdType.MESH


def exchange_kernel(batches, neg_rows, partial_ref, neg_out, pos_out,
                    received, crossing, arrived, slopes, sums,
                    send_a, recv_a, send_x, recv_x, send_b, recv_b, send_c, recv_c):
    me = lax.axis_index("col")
    dom = lax.axis_index("dom")
    pair = me + 1 - 2 * lax.rem(me, 2)
    cross = lax.rem(me + 2, 4)
    far = lax.rem(pair + 2, 4)

    barrier = pltpu.get_barrier_semaphore()
    for other in (pair, cross):
        pl.semaphore_signal(barrier, inc=1, device_id=(dom, other), device_id_type=MESH_ID)
    pl.semaphore_wait(barrier, 2)

    def on_chip(batch, slot, span):
        return pltpu.make_async_remote_copy(
            src_ref=partial_ref.at[span, batch], dst_ref=received.at[slot, batch],
            send_sem=send_a.at[batch * 2 + slot], recv_sem=recv_a.at[batch * 2 + slot],
            device_id=(dom, pair), device_id_type=MESH_ID)

    def across(batch):
        return pltpu.make_async_remote_copy(
            src_ref=crossing.at[batch], dst_ref=arrived.at[batch],
            send_sem=send_x.at[batch], recv_sem=recv_x.at[batch],
            device_id=(dom, cross), device_id_type=MESH_ID)

    def slope_copies(batch, span, dst, route):
        return (
            pltpu.make_async_remote_copy(
                src_ref=slopes.at[span, batch], dst_ref=slopes.at[span, batch],
                send_sem=send_b.at[batch * 3 + route], recv_sem=recv_b.at[batch * 4 + span],
                device_id=(dom, dst), device_id_type=MESH_ID),
            pltpu.make_async_remote_copy(
                src_ref=sums.at[span, batch], dst_ref=sums.at[span, batch],
                send_sem=send_c.at[batch * 3 + route], recv_sem=recv_c.at[batch * 4 + span],
                device_id=(dom, dst), device_id_type=MESH_ID),
        )

    started = []
    for batch in range(batches):
        for copy in (on_chip(batch, 0, pair), on_chip(batch, 1, far)):
            copy.start()
            started.append(copy)
    for batch in range(batches):
        on_chip(batch, 0, me).wait_recv()
        on_chip(batch, 1, cross).wait_recv()
        crossing[batch] = (
            partial_ref[cross, batch].astype(jnp.float32) + received[1, batch].astype(jnp.float32)
        ).astype(crossing.dtype)
        copy = across(batch)
        copy.start()
        started.append(copy)
    for batch in range(batches):
        across(batch).wait_recv()
        total = (
            partial_ref[me, batch].astype(jnp.float32)
            + received[0, batch].astype(jnp.float32)
            + arrived[batch].astype(jnp.float32)
        )
        slopes[me, batch] = (1.0 / (1.0 + jnp.exp(-total[:neg_rows]))).astype(slopes.dtype)
        sums[me, batch] = total[neg_rows:neg_rows + 8]
        for copy in slope_copies(batch, me, cross, 0) + slope_copies(batch, me, pair, 1):
            copy.start()
            started.append(copy)
    for batch in range(batches):
        for copy in slope_copies(batch, cross, me, 0):
            copy.wait_recv()
        for copy in slope_copies(batch, cross, pair, 2):
            copy.start()
            started.append(copy)
    for batch in range(batches):
        for copy in slope_copies(batch, pair, me, 1) + slope_copies(batch, far, me, 2):
            copy.wait_recv()
    for copy in started:
        copy.wait_send()
    neg_out[...] = slopes[...]
    pos_out[...] = sums[...]


def col_exchange(partial):
    parts, batches, rows, lanes = partial.shape
    neg_rows = rows - 16
    vmem = pl.BlockSpec(memory_space=pltpu.VMEM)
    return pl.pallas_call(
        functools.partial(exchange_kernel, batches, neg_rows),
        out_shape=(
            jax.ShapeDtypeStruct((parts, batches, neg_rows, lanes), jnp.bfloat16),
            jax.ShapeDtypeStruct((parts, batches, 8, lanes), jnp.float32),
        ),
        in_specs=[vmem],
        out_specs=(vmem, vmem),
        scratch_shapes=[
            pltpu.VMEM((2, batches, rows, lanes), jnp.bfloat16),
            pltpu.VMEM((batches, rows, lanes), jnp.bfloat16),
            pltpu.VMEM((batches, rows, lanes), jnp.bfloat16),
            pltpu.VMEM((parts, batches, neg_rows, lanes), jnp.bfloat16),
            pltpu.VMEM((parts, batches, 8, lanes), jnp.float32),
            pltpu.SemaphoreType.DMA((2 * batches,)),
            pltpu.SemaphoreType.DMA((2 * batches,)),
            pltpu.SemaphoreType.DMA((batches,)),
            pltpu.SemaphoreType.DMA((batches,)),
            pltpu.SemaphoreType.DMA((3 * batches,)),
            pltpu.SemaphoreType.DMA((parts * batches,)),
            pltpu.SemaphoreType.DMA((3 * batches,)),
            pltpu.SemaphoreType.DMA((parts * batches,)),
        ],
        compiler_params=pltpu.CompilerParams(
            collective_id=0, has_side_effects=True, vmem_limit_bytes=48 * 1024 * 1024
        ),
    )(partial)


def shifted(shard, axis, by):
    size = lax.axis_size(axis)
    return lax.ppermute(shard, axis, [(i, (i + by) % size) for i in range(size)])


def gather_cols(table, indices):
    count = table.shape[1]
    one_hot = (
        lax.broadcasted_iota(jnp.int32, (count, indices.shape[0]), 0) == indices[None, :]
    ).astype(table.dtype)
    return jnp.dot(table, one_hot, preferred_element_type=jnp.float32)


def split_exact(values):
    high = values.astype(jnp.bfloat16)
    low = (values - high.astype(jnp.float32)).astype(jnp.bfloat16)
    return high, low


def scatter_rows(values, indices, count):
    one_hot = (
        lax.broadcasted_iota(jnp.int32, (count, indices.shape[0]), 0) == indices[None, :]
    ).astype(jnp.bfloat16)
    return lax.dot_general(
        one_hot, values, (((1,), (1,)), ((), ())), preferred_element_type=jnp.float32
    )


def scatter_f32(values, indices, count):
    rows = values.shape[0]
    high, low = split_exact(values)
    summed = scatter_rows(jnp.concatenate([high, low], axis=0), indices, count)
    return summed[:, :rows] + summed[:, rows:]


def body(embeddings, relations, source_ids, relation_ids, target_ids, negative_ids, served_rows):
    halves, columns, entities = embeddings.shape
    flat_width = halves * columns
    buckets, edge_count = source_ids.shape
    spans, negs_per = (negative_ids.shape[1], negative_ids.shape[2])
    span_len = edge_count // spans
    table = embeddings.reshape(flat_width, entities)
    relation_flat = relations.reshape(flat_width, relations.shape[2])
    served_flat = served_rows.reshape(-1)

    asked = [None] + [shifted(target_ids[b], "dom", -b) for b in range(1, buckets)]
    fetched = gather_cols(table, served_flat).astype(jnp.bfloat16)
    serving = [gather_cols(table, asked[b]).astype(jnp.bfloat16) for b in range(1, buckets)]
    table, *serving = lax.optimization_barrier((table, *serving))
    answered = [None] + [shifted(serving[b - 1], "dom", b) for b in range(1, buckets)]

    negative_pool = lax.all_to_all(
        fetched.reshape(halves, columns, -1), "dom", split_axis=2, concat_axis=2, tiled=True
    )
    pool_flat = negative_pool.reshape(flat_width, -1)
    pool_count = pool_flat.shape[1]

    local_ids = jnp.concatenate([source_ids.reshape(-1), target_ids[0]])
    local_hot = (
        lax.broadcasted_iota(jnp.int32, (local_ids.shape[0], entities), 1) == local_ids[:, None]
    ).astype(table.dtype)
    local_rows = lax.dot_general(
        local_hot, table, (((1,), (1,)), ((), ())), preferred_element_type=jnp.float32
    ).T

    def scores(bucket):
        negative_flat = negative_ids[bucket].reshape(-1)
        source_rows = local_rows[:, bucket * edge_count:(bucket + 1) * edge_count].reshape(
            halves, columns, edge_count
        )
        relation_rows = gather_cols(relation_flat, relation_ids[bucket]).reshape(
            halves, columns, edge_count
        )
        if bucket == 0:
            target_half = local_rows[:, buckets * edge_count:]
        else:
            target_half = answered[bucket].astype(jnp.float32)
        target_rows = target_half.reshape(halves, columns, edge_count)
        product = jnp.stack(
            [
                source_rows[0] * relation_rows[0] - source_rows[1] * relation_rows[1],
                source_rows[0] * relation_rows[1] + source_rows[1] * relation_rows[0],
            ]
        )
        rounded = product.astype(jnp.bfloat16)
        rounded_wide = rounded.astype(jnp.float32)
        positive_part = jnp.sum(rounded_wide * target_rows, axis=(0, 1))
        negative_rows = gather_cols(pool_flat, negative_flat).astype(jnp.bfloat16).reshape(
            flat_width, spans, negs_per
        )
        query_rows = rounded.reshape(flat_width, spans, span_len)
        negative_part = lax.dot_general(
            query_rows,
            negative_rows,
            (((0,), (0,)), ((1,), (1,))),
            preferred_element_type=jnp.float32,
        ).reshape(spans, -1, 128)
        positive_rows = positive_part.reshape(spans, -1, 128)
        pad = jnp.zeros((spans, 16 - positive_rows.shape[1], 128), jnp.float32)
        partial = jnp.concatenate([negative_part, positive_rows, pad], axis=1).astype(
            jnp.bfloat16
        )
        state = (relation_rows, target_rows, rounded, rounded_wide, negative_rows, query_rows)
        return partial, state

    def gradients(bucket, reduced, state):
        relation_rows, target_rows, rounded, rounded_wide, negative_rows, query_rows = state
        negative_slope, positive_sums = reduced
        positive = positive_sums[:, : span_len // 128].reshape(edge_count)
        positive_slope = -jax.nn.sigmoid(-positive)
        slope_spans = negative_slope.reshape(spans, span_len, negs_per)
        pool_terms = lax.dot_general(
            query_rows,
            slope_spans,
            (((2,), (1,)), ((1,), (0,))),
            preferred_element_type=jnp.float32,
        ).transpose(1, 0, 2).reshape(flat_width, spans * negs_per)
        query_terms = lax.dot_general(
            slope_spans,
            negative_rows,
            (((2,), (2,)), ((0,), (1,))),
            preferred_element_type=jnp.float32,
        )
        query_terms = query_terms.transpose(2, 0, 1).reshape(halves, columns, edge_count)
        total_grad = positive_slope * target_rows + query_terms
        target_values = (positive_slope * rounded_wide).reshape(flat_width, edge_count)
        source_grad = jnp.stack(
            [
                total_grad[0] * relation_rows[0] + total_grad[1] * relation_rows[1],
                total_grad[1] * relation_rows[0] - total_grad[0] * relation_rows[1],
            ]
        ).reshape(flat_width, edge_count)
        return pool_terms, target_values, source_grad

    owned = jnp.zeros((entities, flat_width), jnp.float32)
    pool_values, pool_index = [], []
    bf16_values, bf16_index = [], []
    results = [scores(bucket) for bucket in range(buckets)]
    negative_all, positive_all = col_exchange(jnp.stack([r[0] for r in results], axis=1))
    for done in range(buckets):
        reduced = (negative_all[:, done], positive_all[:, done])
        pool_terms, target_values, source_grad = gradients(done, reduced, results[done][1])
        pool_values.append(pool_terms)
        pool_index.append(negative_ids[done].reshape(-1))
        if done == 0:
            owned = owned + scatter_f32(
                jnp.concatenate([source_grad, target_values], axis=1),
                jnp.concatenate([source_ids[0], target_ids[0]]),
                entities,
            )
        else:
            owned = owned + scatter_f32(source_grad, source_ids[done], entities)
            bf16_values.append(shifted(target_values.astype(jnp.bfloat16), "dom", -done))
            bf16_index.append(asked[done])

    pool_grad = scatter_f32(
        jnp.concatenate(pool_values, axis=1), jnp.concatenate(pool_index), pool_count
    ).T
    returned = lax.all_to_all(
        pool_grad.reshape(halves, columns, -1).astype(jnp.bfloat16),
        "dom",
        split_axis=2,
        concat_axis=2,
        tiled=True,
    ).reshape(flat_width, -1)
    bf16_values.append(returned)
    bf16_index.append(served_flat)
    owned = owned + scatter_rows(
        jnp.concatenate(bf16_values, axis=1), jnp.concatenate(bf16_index), entities
    )
    return owned.T.reshape(halves, columns, entities)


def solution(mesh):
    placed = (
        P(None, "col", "dom"),
        P(None, "col", None),
        P(None, "dom"),
        P(None, "dom"),
        P(None, "dom"),
        P(None, "dom", None),
        P("dom", None),
    )
    return jax.shard_map(
        body, mesh=mesh, in_specs=placed, out_specs=P(None, "col", "dom"), check_vma=False
    )
```

```python
import functools

import jax
import jax.numpy as jnp
from jax import lax
from jax.experimental import pallas as pl
from jax.experimental.pallas import tpu as pltpu
from jax.sharding import PartitionSpec as P

MESH_ID = pl.DeviceIdType.MESH


def exchange_kernel(batches, neg_rows, partial_ref, neg_out, pos_out,
                    received, crossing, arrived, slopes, sums,
                    send_a, recv_a, send_x, recv_x, send_b, recv_b, send_c, recv_c):
    me = lax.axis_index("col")
    dom = lax.axis_index("dom")
    pair = me + 1 - 2 * lax.rem(me, 2)
    cross = lax.rem(me + 2, 4)
    far = lax.rem(pair + 2, 4)

    barrier = pltpu.get_barrier_semaphore()
    for other in (pair, cross):
        pl.semaphore_signal(barrier, inc=1, device_id=(dom, other), device_id_type=MESH_ID)
    pl.semaphore_wait(barrier, 2)

    def on_chip(batch, slot, span):
        return pltpu.make_async_remote_copy(
            src_ref=partial_ref.at[span, batch], dst_ref=received.at[slot, batch],
            send_sem=send_a.at[batch * 2 + slot], recv_sem=recv_a.at[batch * 2 + slot],
            device_id=(dom, pair), device_id_type=MESH_ID)

    def across(batch):
        return pltpu.make_async_remote_copy(
            src_ref=crossing.at[batch], dst_ref=arrived.at[batch],
            send_sem=send_x.at[batch], recv_sem=recv_x.at[batch],
            device_id=(dom, cross), device_id_type=MESH_ID)

    def slope_copies(batch, span, dst, route):
        return (
            pltpu.make_async_remote_copy(
                src_ref=slopes.at[span, batch], dst_ref=slopes.at[span, batch],
                send_sem=send_b.at[batch * 3 + route], recv_sem=recv_b.at[batch * 4 + span],
                device_id=(dom, dst), device_id_type=MESH_ID),
            pltpu.make_async_remote_copy(
                src_ref=sums.at[span, batch], dst_ref=sums.at[span, batch],
                send_sem=send_c.at[batch * 3 + route], recv_sem=recv_c.at[batch * 4 + span],
                device_id=(dom, dst), device_id_type=MESH_ID),
        )

    started = []
    for batch in range(batches):
        for copy in (on_chip(batch, 0, pair), on_chip(batch, 1, far)):
            copy.start()
            started.append(copy)
    for batch in range(batches):
        on_chip(batch, 0, me).wait_recv()
        on_chip(batch, 1, cross).wait_recv()
        crossing[batch] = (
            partial_ref[cross, batch].astype(jnp.float32) + received[1, batch].astype(jnp.float32)
        ).astype(crossing.dtype)
        copy = across(batch)
        copy.start()
        started.append(copy)
    for batch in range(batches):
        across(batch).wait_recv()
        total = (
            partial_ref[me, batch].astype(jnp.float32)
            + received[0, batch].astype(jnp.float32)
            + arrived[batch].astype(jnp.float32)
        )
        slopes[me, batch] = (1.0 / (1.0 + jnp.exp(-total[:neg_rows]))).astype(slopes.dtype)
        sums[me, batch] = total[neg_rows:neg_rows + 8]
        for copy in slope_copies(batch, me, cross, 0) + slope_copies(batch, me, pair, 1):
            copy.start()
            started.append(copy)
    for batch in range(batches):
        for copy in slope_copies(batch, cross, me, 0):
            copy.wait_recv()
        for copy in slope_copies(batch, cross, pair, 2):
            copy.start()
            started.append(copy)
    for batch in range(batches):
        for copy in slope_copies(batch, pair, me, 1) + slope_copies(batch, far, me, 2):
            copy.wait_recv()
    for copy in started:
        copy.wait_send()
    neg_out[...] = slopes[...]
    pos_out[...] = sums[...]


def col_exchange(partial):
    parts, batches, rows, lanes = partial.shape
    neg_rows = rows - 16
    vmem = pl.BlockSpec(memory_space=pltpu.VMEM)
    return pl.pallas_call(
        functools.partial(exchange_kernel, batches, neg_rows),
        out_shape=(
            jax.ShapeDtypeStruct((parts, batches, neg_rows, lanes), jnp.bfloat16),
            jax.ShapeDtypeStruct((parts, batches, 8, lanes), jnp.float32),
        ),
        in_specs=[vmem],
        out_specs=(vmem, vmem),
        scratch_shapes=[
            pltpu.VMEM((2, batches, rows, lanes), jnp.bfloat16),
            pltpu.VMEM((batches, rows, lanes), jnp.bfloat16),
            pltpu.VMEM((batches, rows, lanes), jnp.bfloat16),
            pltpu.VMEM((parts, batches, neg_rows, lanes), jnp.bfloat16),
            pltpu.VMEM((parts, batches, 8, lanes), jnp.float32),
            pltpu.SemaphoreType.DMA((2 * batches,)),
            pltpu.SemaphoreType.DMA((2 * batches,)),
            pltpu.SemaphoreType.DMA((batches,)),
            pltpu.SemaphoreType.DMA((batches,)),
            pltpu.SemaphoreType.DMA((3 * batches,)),
            pltpu.SemaphoreType.DMA((parts * batches,)),
            pltpu.SemaphoreType.DMA((3 * batches,)),
            pltpu.SemaphoreType.DMA((parts * batches,)),
        ],
        compiler_params=pltpu.CompilerParams(
            collective_id=0, has_side_effects=True, vmem_limit_bytes=48 * 1024 * 1024
        ),
    )(partial)


def shifted(shard, axis, by):
    size = lax.axis_size(axis)
    return lax.ppermute(shard, axis, [(i, (i + by) % size) for i in range(size)])


def gather_cols(table, indices):
    count = table.shape[1]
    one_hot = (
        lax.broadcasted_iota(jnp.int32, (count, indices.shape[0]), 0) == indices[None, :]
    ).astype(table.dtype)
    return jnp.dot(table, one_hot, preferred_element_type=jnp.float32)


def split_exact(values):
    high = values.astype(jnp.bfloat16)
    low = (values - high.astype(jnp.float32)).astype(jnp.bfloat16)
    return high, low


def scatter_rows(values, indices, count):
    one_hot = (
        lax.broadcasted_iota(jnp.int32, (count, indices.shape[0]), 0) == indices[None, :]
    ).astype(jnp.bfloat16)
    return lax.dot_general(
        one_hot, values, (((1,), (1,)), ((), ())), preferred_element_type=jnp.float32
    )


def scatter_f32(values, indices, count):
    rows = values.shape[0]
    high, low = split_exact(values)
    summed = scatter_rows(jnp.concatenate([high, low], axis=0), indices, count)
    return summed[:, :rows] + summed[:, rows:]


def body(embeddings, relations, source_ids, relation_ids, target_ids, negative_ids, served_rows):
    halves, columns, entities = embeddings.shape
    flat_width = halves * columns
    buckets, edge_count = source_ids.shape
    spans, negs_per = (negative_ids.shape[1], negative_ids.shape[2])
    span_len = edge_count // spans
    table = embeddings.reshape(flat_width, entities)
    relation_flat = relations.reshape(flat_width, relations.shape[2])
    served_flat = served_rows.reshape(-1)

    asked = [None] + [shifted(target_ids[b], "dom", -b) for b in range(1, buckets)]
    fetched = gather_cols(table, served_flat).astype(jnp.bfloat16)
    serving = [gather_cols(table, asked[b]).astype(jnp.bfloat16) for b in range(1, buckets)]
    table, *serving = lax.optimization_barrier((table, *serving))
    answered = [None] + [shifted(serving[b - 1], "dom", b) for b in range(1, buckets)]

    negative_pool = lax.all_to_all(
        fetched.reshape(halves, columns, -1), "dom", split_axis=2, concat_axis=2, tiled=True
    )
    pool_flat = negative_pool.reshape(flat_width, -1)
    pool_count = pool_flat.shape[1]

    def scores(bucket):
        negative_flat = negative_ids[bucket].reshape(-1)
        source_rows = gather_cols(table, source_ids[bucket]).reshape(halves, columns, edge_count)
        relation_rows = gather_cols(relation_flat, relation_ids[bucket]).reshape(
            halves, columns, edge_count
        )
        if bucket == 0:
            target_half = gather_cols(table, target_ids[0])
        else:
            target_half = answered[bucket].astype(jnp.float32)
        target_rows = target_half.reshape(halves, columns, edge_count)
        product = jnp.stack(
            [
                source_rows[0] * relation_rows[0] - source_rows[1] * relation_rows[1],
                source_rows[0] * relation_rows[1] + source_rows[1] * relation_rows[0],
            ]
        )
        rounded = product.astype(jnp.bfloat16)
        rounded_wide = rounded.astype(jnp.float32)
        positive_part = jnp.dot(
            jnp.ones((1, flat_width), jnp.float32),
            (rounded_wide * target_rows).reshape(flat_width, edge_count),
            precision=lax.Precision.HIGHEST,
            preferred_element_type=jnp.float32,
        ).reshape(edge_count)
        negative_rows = gather_cols(pool_flat, negative_flat).astype(jnp.bfloat16).reshape(
            flat_width, spans, negs_per
        )
        query_rows = rounded.reshape(flat_width, spans, span_len)
        negative_part = lax.dot_general(
            query_rows,
            negative_rows,
            (((0,), (0,)), ((1,), (1,))),
            preferred_element_type=jnp.float32,
        ).reshape(spans, -1, 128)
        positive_rows = positive_part.reshape(spans, -1, 128)
        pad = jnp.zeros((spans, 16 - positive_rows.shape[1], 128), jnp.float32)
        partial = jnp.concatenate([negative_part, positive_rows, pad], axis=1).astype(
            jnp.bfloat16
        )
        state = (relation_rows, target_rows, rounded, rounded_wide, negative_rows, query_rows)
        return partial, state

    def gradients(bucket, reduced, state):
        relation_rows, target_rows, rounded, rounded_wide, negative_rows, query_rows = state
        negative_slope, positive_sums = reduced
        positive = positive_sums[:, : span_len // 128].reshape(edge_count)
        positive_slope = -jax.nn.sigmoid(-positive)
        slope_spans = negative_slope.reshape(spans, span_len, negs_per)
        pool_terms = lax.dot_general(
            query_rows,
            slope_spans,
            (((2,), (1,)), ((1,), (0,))),
            preferred_element_type=jnp.float32,
        ).transpose(1, 0, 2).reshape(flat_width, spans * negs_per)
        query_terms = lax.dot_general(
            slope_spans,
            negative_rows,
            (((2,), (2,)), ((0,), (1,))),
            preferred_element_type=jnp.float32,
        )
        query_terms = query_terms.transpose(2, 0, 1).reshape(halves, columns, edge_count)
        total_grad = positive_slope * target_rows + query_terms
        target_values = (positive_slope * rounded_wide).reshape(flat_width, edge_count)
        source_grad = jnp.stack(
            [
                total_grad[0] * relation_rows[0] + total_grad[1] * relation_rows[1],
                total_grad[1] * relation_rows[0] - total_grad[0] * relation_rows[1],
            ]
        ).reshape(flat_width, edge_count)
        return pool_terms, target_values, source_grad

    owned = jnp.zeros((entities, flat_width), jnp.float32)
    pool_values, pool_index = [], []
    bf16_values, bf16_index = [], []
    results = [scores(bucket) for bucket in range(buckets)]
    negative_all, positive_all = col_exchange(jnp.stack([r[0] for r in results], axis=1))
    for done in range(buckets):
        reduced = (negative_all[:, done], positive_all[:, done])
        pool_terms, target_values, source_grad = gradients(done, reduced, results[done][1])
        pool_values.append(pool_terms)
        pool_index.append(negative_ids[done].reshape(-1))
        if done == 0:
            owned = owned + scatter_f32(
                jnp.concatenate([source_grad, target_values], axis=1),
                jnp.concatenate([source_ids[0], target_ids[0]]),
                entities,
            )
        else:
            owned = owned + scatter_f32(source_grad, source_ids[done], entities)
            bf16_values.append(shifted(target_values.astype(jnp.bfloat16), "dom", -done))
            bf16_index.append(asked[done])

    pool_grad = scatter_f32(
        jnp.concatenate(pool_values, axis=1), jnp.concatenate(pool_index), pool_count
    ).T
    returned = lax.all_to_all(
        pool_grad.reshape(halves, columns, -1).astype(jnp.bfloat16),
        "dom",
        split_axis=2,
        concat_axis=2,
        tiled=True,
    ).reshape(flat_width, -1)
    bf16_values.append(returned)
    bf16_index.append(served_flat)
    owned = owned + scatter_rows(
        jnp.concatenate(bf16_values, axis=1), jnp.concatenate(bf16_index), entities
    )
    return owned.T.reshape(halves, columns, entities)


def solution(mesh):
    placed = (
        P(None, "col", "dom"),
        P(None, "col", None),
        P(None, "dom"),
        P(None, "dom"),
        P(None, "dom"),
        P(None, "dom", None),
        P("dom", None),
    )
    return jax.shard_map(
        body, mesh=mesh, in_specs=placed, out_specs=P(None, "col", "dom"), check_vma=False
    )
```

```python
import functools

import jax
import jax.numpy as jnp
from jax import lax
from jax.experimental import pallas as pl
from jax.experimental.pallas import tpu as pltpu
from jax.sharding import PartitionSpec as P

MESH_ID = pl.DeviceIdType.MESH


def exchange_kernel(batches, neg_rows, partial_ref, neg_out, pos_out,
                    received, crossing, arrived, slopes, sums,
                    send_a, recv_a, send_x, recv_x, send_b, recv_b, send_c, recv_c):
    me = lax.axis_index("col")
    dom = lax.axis_index("dom")
    pair = me + 1 - 2 * lax.rem(me, 2)
    cross = lax.rem(me + 2, 4)
    far = lax.rem(pair + 2, 4)

    barrier = pltpu.get_barrier_semaphore()
    for other in (pair, cross):
        pl.semaphore_signal(barrier, inc=1, device_id=(dom, other), device_id_type=MESH_ID)
    pl.semaphore_wait(barrier, 2)

    def on_chip(batch, slot, span):
        return pltpu.make_async_remote_copy(
            src_ref=partial_ref.at[span, batch], dst_ref=received.at[slot, batch],
            send_sem=send_a.at[batch * 2 + slot], recv_sem=recv_a.at[batch * 2 + slot],
            device_id=(dom, pair), device_id_type=MESH_ID)

    def across(batch):
        return pltpu.make_async_remote_copy(
            src_ref=crossing.at[batch], dst_ref=arrived.at[batch],
            send_sem=send_x.at[batch], recv_sem=recv_x.at[batch],
            device_id=(dom, cross), device_id_type=MESH_ID)

    def slope_copies(batch, span, dst, route):
        return (
            pltpu.make_async_remote_copy(
                src_ref=slopes.at[span, batch], dst_ref=slopes.at[span, batch],
                send_sem=send_b.at[batch * 3 + route], recv_sem=recv_b.at[batch * 4 + span],
                device_id=(dom, dst), device_id_type=MESH_ID),
            pltpu.make_async_remote_copy(
                src_ref=sums.at[span, batch], dst_ref=sums.at[span, batch],
                send_sem=send_c.at[batch * 3 + route], recv_sem=recv_c.at[batch * 4 + span],
                device_id=(dom, dst), device_id_type=MESH_ID),
        )

    started = []
    for batch in range(batches):
        for copy in (on_chip(batch, 0, pair), on_chip(batch, 1, far)):
            copy.start()
            started.append(copy)
    for batch in range(batches):
        on_chip(batch, 1, cross).wait_recv()
        crossing[batch] = (
            partial_ref[cross, batch].astype(jnp.float32) + received[1, batch].astype(jnp.float32)
        ).astype(crossing.dtype)
        copy = across(batch)
        copy.start()
        started.append(copy)
    for batch in range(batches):
        on_chip(batch, 0, me).wait_recv()
        across(batch).wait_recv()
        total = (
            partial_ref[me, batch].astype(jnp.float32)
            + received[0, batch].astype(jnp.float32)
            + arrived[batch].astype(jnp.float32)
        )
        slopes[me, batch] = (1.0 / (1.0 + jnp.exp(-total[:neg_rows]))).astype(slopes.dtype)
        sums[me, batch] = total[neg_rows:neg_rows + 8]
        for copy in slope_copies(batch, me, cross, 0) + slope_copies(batch, me, pair, 1):
            copy.start()
            started.append(copy)
    for batch in range(batches):
        for copy in slope_copies(batch, cross, me, 0):
            copy.wait_recv()
        for copy in slope_copies(batch, cross, pair, 2):
            copy.start()
            started.append(copy)
    for batch in range(batches):
        for copy in slope_copies(batch, pair, me, 1) + slope_copies(batch, far, me, 2):
            copy.wait_recv()
    for copy in started:
        copy.wait_send()
    neg_out[...] = slopes[...]
    pos_out[...] = sums[...]


def col_exchange(partial):
    parts, batches, rows, lanes = partial.shape
    neg_rows = rows - 16
    vmem = pl.BlockSpec(memory_space=pltpu.VMEM)
    return pl.pallas_call(
        functools.partial(exchange_kernel, batches, neg_rows),
        out_shape=(
            jax.ShapeDtypeStruct((parts, batches, neg_rows, lanes), jnp.bfloat16),
            jax.ShapeDtypeStruct((parts, batches, 8, lanes), jnp.float32),
        ),
        in_specs=[vmem],
        out_specs=(vmem, vmem),
        scratch_shapes=[
            pltpu.VMEM((2, batches, rows, lanes), jnp.bfloat16),
            pltpu.VMEM((batches, rows, lanes), jnp.bfloat16),
            pltpu.VMEM((batches, rows, lanes), jnp.bfloat16),
            pltpu.VMEM((parts, batches, neg_rows, lanes), jnp.bfloat16),
            pltpu.VMEM((parts, batches, 8, lanes), jnp.float32),
            pltpu.SemaphoreType.DMA((2 * batches,)),
            pltpu.SemaphoreType.DMA((2 * batches,)),
            pltpu.SemaphoreType.DMA((batches,)),
            pltpu.SemaphoreType.DMA((batches,)),
            pltpu.SemaphoreType.DMA((3 * batches,)),
            pltpu.SemaphoreType.DMA((parts * batches,)),
            pltpu.SemaphoreType.DMA((3 * batches,)),
            pltpu.SemaphoreType.DMA((parts * batches,)),
        ],
        compiler_params=pltpu.CompilerParams(
            collective_id=0, has_side_effects=True, vmem_limit_bytes=48 * 1024 * 1024
        ),
    )(partial)


def shifted(shard, axis, by):
    size = lax.axis_size(axis)
    return lax.ppermute(shard, axis, [(i, (i + by) % size) for i in range(size)])


def gather_cols(table, indices):
    count = table.shape[1]
    one_hot = (
        lax.broadcasted_iota(jnp.int32, (count, indices.shape[0]), 0) == indices[None, :]
    ).astype(table.dtype)
    return jnp.dot(table, one_hot, preferred_element_type=jnp.float32)


def split_exact(values):
    high = values.astype(jnp.bfloat16)
    low = (values - high.astype(jnp.float32)).astype(jnp.bfloat16)
    return high, low


def scatter_rows(values, indices, count):
    one_hot = (
        lax.broadcasted_iota(jnp.int32, (count, indices.shape[0]), 0) == indices[None, :]
    ).astype(jnp.bfloat16)
    return lax.dot_general(
        one_hot, values, (((1,), (1,)), ((), ())), preferred_element_type=jnp.float32
    )


def scatter_f32(values, indices, count):
    rows = values.shape[0]
    high, low = split_exact(values)
    summed = scatter_rows(jnp.concatenate([high, low], axis=0), indices, count)
    return summed[:, :rows] + summed[:, rows:]


def body(embeddings, relations, source_ids, relation_ids, target_ids, negative_ids, served_rows):
    halves, columns, entities = embeddings.shape
    flat_width = halves * columns
    buckets, edge_count = source_ids.shape
    spans, negs_per = (negative_ids.shape[1], negative_ids.shape[2])
    span_len = edge_count // spans
    table = embeddings.reshape(flat_width, entities)
    relation_flat = relations.reshape(flat_width, relations.shape[2])
    served_flat = served_rows.reshape(-1)

    asked = [None] + [shifted(target_ids[b], "dom", -b) for b in range(1, buckets)]
    fetched = gather_cols(table, served_flat).astype(jnp.bfloat16)
    serving = [gather_cols(table, asked[b]).astype(jnp.bfloat16) for b in range(1, buckets)]
    table, *serving = lax.optimization_barrier((table, *serving))
    answered = [None] + [shifted(serving[b - 1], "dom", b) for b in range(1, buckets)]

    negative_pool = lax.all_to_all(
        fetched.reshape(halves, columns, -1), "dom", split_axis=2, concat_axis=2, tiled=True
    )
    pool_flat = negative_pool.reshape(flat_width, -1)
    pool_count = pool_flat.shape[1]

    def scores(bucket):
        negative_flat = negative_ids[bucket].reshape(-1)
        source_rows = gather_cols(table, source_ids[bucket]).reshape(halves, columns, edge_count)
        relation_rows = gather_cols(relation_flat, relation_ids[bucket]).reshape(
            halves, columns, edge_count
        )
        if bucket == 0:
            target_half = gather_cols(table, target_ids[0])
        else:
            target_half = answered[bucket].astype(jnp.float32)
        target_rows = target_half.reshape(halves, columns, edge_count)
        product = jnp.stack(
            [
                source_rows[0] * relation_rows[0] - source_rows[1] * relation_rows[1],
                source_rows[0] * relation_rows[1] + source_rows[1] * relation_rows[0],
            ]
        )
        rounded = product.astype(jnp.bfloat16)
        rounded_wide = rounded.astype(jnp.float32)
        positive_part = jnp.sum(rounded_wide * target_rows, axis=(0, 1))
        negative_rows = gather_cols(pool_flat, negative_flat).astype(jnp.bfloat16).reshape(
            flat_width, spans, negs_per
        )
        query_rows = rounded.reshape(flat_width, spans, span_len)
        negative_part = lax.dot_general(
            query_rows,
            negative_rows,
            (((0,), (0,)), ((1,), (1,))),
            preferred_element_type=jnp.float32,
        ).reshape(spans, -1, 128)
        positive_rows = positive_part.reshape(spans, -1, 128)
        pad = jnp.zeros((spans, 16 - positive_rows.shape[1], 128), jnp.float32)
        partial = jnp.concatenate([negative_part, positive_rows, pad], axis=1).astype(
            jnp.bfloat16
        )
        state = (relation_rows, target_rows, rounded, rounded_wide, negative_rows, query_rows)
        return partial, state

    def gradients(bucket, reduced, state):
        relation_rows, target_rows, rounded, rounded_wide, negative_rows, query_rows = state
        negative_slope, positive_sums = reduced
        positive = positive_sums[:, : span_len // 128].reshape(edge_count)
        positive_slope = -jax.nn.sigmoid(-positive)
        slope_spans = negative_slope.reshape(spans, span_len, negs_per)
        pool_terms = lax.dot_general(
            query_rows,
            slope_spans,
            (((2,), (1,)), ((1,), (0,))),
            preferred_element_type=jnp.float32,
        ).transpose(1, 0, 2).reshape(flat_width, spans * negs_per)
        query_terms = lax.dot_general(
            slope_spans,
            negative_rows,
            (((2,), (2,)), ((0,), (1,))),
            preferred_element_type=jnp.float32,
        )
        query_terms = query_terms.transpose(2, 0, 1).reshape(halves, columns, edge_count)
        total_grad = positive_slope * target_rows + query_terms
        target_values = (positive_slope * rounded_wide).reshape(flat_width, edge_count)
        source_grad = jnp.stack(
            [
                total_grad[0] * relation_rows[0] + total_grad[1] * relation_rows[1],
                total_grad[1] * relation_rows[0] - total_grad[0] * relation_rows[1],
            ]
        ).reshape(flat_width, edge_count)
        return pool_terms, target_values, source_grad

    owned = jnp.zeros((entities, flat_width), jnp.float32)
    pool_values, pool_index = [], []
    bf16_values, bf16_index = [], []
    results = [scores(bucket) for bucket in range(buckets)]
    negative_all, positive_all = col_exchange(jnp.stack([r[0] for r in results], axis=1))
    for done in range(buckets):
        reduced = (negative_all[:, done], positive_all[:, done])
        pool_terms, target_values, source_grad = gradients(done, reduced, results[done][1])
        pool_values.append(pool_terms)
        pool_index.append(negative_ids[done].reshape(-1))
        if done == 0:
            owned = owned + scatter_f32(
                jnp.concatenate([source_grad, target_values], axis=1),
                jnp.concatenate([source_ids[0], target_ids[0]]),
                entities,
            )
        else:
            owned = owned + scatter_f32(source_grad, source_ids[done], entities)
            bf16_values.append(shifted(target_values.astype(jnp.bfloat16), "dom", -done))
            bf16_index.append(asked[done])

    pool_grad = scatter_f32(
        jnp.concatenate(pool_values, axis=1), jnp.concatenate(pool_index), pool_count
    ).T
    returned = lax.all_to_all(
        pool_grad.reshape(halves, columns, -1).astype(jnp.bfloat16),
        "dom",
        split_axis=2,
        concat_axis=2,
        tiled=True,
    ).reshape(flat_width, -1)
    bf16_values.append(returned)
    bf16_index.append(served_flat)
    owned = owned + scatter_rows(
        jnp.concatenate(bf16_values, axis=1), jnp.concatenate(bf16_index), entities
    )
    return owned.T.reshape(halves, columns, entities)


def solution(mesh):
    placed = (
        P(None, "col", "dom"),
        P(None, "col", None),
        P(None, "dom"),
        P(None, "dom"),
        P(None, "dom"),
        P(None, "dom", None),
        P("dom", None),
    )
    return jax.shard_map(
        body, mesh=mesh, in_specs=placed, out_specs=P(None, "col", "dom"), check_vma=False
    )
```

```python
import functools

import jax
import jax.numpy as jnp
from jax import lax
from jax.experimental import pallas as pl
from jax.experimental.pallas import tpu as pltpu
from jax.sharding import PartitionSpec as P

MESH_ID = pl.DeviceIdType.MESH


def exchange_kernel(batches, neg_rows, partial_ref, slopes, sums,
                    received, crossing, arrived,
                    send_a, recv_a, send_x, recv_x, send_b, recv_b, send_c, recv_c):
    me = lax.axis_index("col")
    dom = lax.axis_index("dom")
    pair = me + 1 - 2 * lax.rem(me, 2)
    cross = lax.rem(me + 2, 4)
    far = lax.rem(pair + 2, 4)

    barrier = pltpu.get_barrier_semaphore()
    for other in (pair, cross):
        pl.semaphore_signal(barrier, inc=1, device_id=(dom, other), device_id_type=MESH_ID)
    pl.semaphore_wait(barrier, 2)

    def on_chip(batch, slot, span):
        return pltpu.make_async_remote_copy(
            src_ref=partial_ref.at[span, batch], dst_ref=received.at[slot, batch],
            send_sem=send_a.at[batch * 2 + slot], recv_sem=recv_a.at[batch * 2 + slot],
            device_id=(dom, pair), device_id_type=MESH_ID)

    def across(batch):
        return pltpu.make_async_remote_copy(
            src_ref=crossing.at[batch], dst_ref=arrived.at[batch],
            send_sem=send_x.at[batch], recv_sem=recv_x.at[batch],
            device_id=(dom, cross), device_id_type=MESH_ID)

    def slope_copies(batch, span, dst, route):
        return (
            pltpu.make_async_remote_copy(
                src_ref=slopes.at[span, batch], dst_ref=slopes.at[span, batch],
                send_sem=send_b.at[batch * 3 + route], recv_sem=recv_b.at[batch * 4 + span],
                device_id=(dom, dst), device_id_type=MESH_ID),
            pltpu.make_async_remote_copy(
                src_ref=sums.at[span, batch], dst_ref=sums.at[span, batch],
                send_sem=send_c.at[batch * 3 + route], recv_sem=recv_c.at[batch * 4 + span],
                device_id=(dom, dst), device_id_type=MESH_ID),
        )

    started = []
    for batch in range(batches):
        for copy in (on_chip(batch, 0, pair), on_chip(batch, 1, far)):
            copy.start()
            started.append(copy)
    for batch in range(batches):
        on_chip(batch, 1, cross).wait_recv()
        crossing[batch] = (
            partial_ref[cross, batch].astype(jnp.float32) + received[1, batch].astype(jnp.float32)
        ).astype(crossing.dtype)
        copy = across(batch)
        copy.start()
        started.append(copy)
    for batch in range(batches):
        on_chip(batch, 0, me).wait_recv()
        across(batch).wait_recv()
        total = (
            partial_ref[me, batch].astype(jnp.float32)
            + received[0, batch].astype(jnp.float32)
            + arrived[batch].astype(jnp.float32)
        )
        slopes[me, batch] = (1.0 / (1.0 + jnp.exp(-total[:neg_rows]))).astype(slopes.dtype)
        sums[me, batch] = total[neg_rows:neg_rows + 8]
        for copy in slope_copies(batch, me, cross, 0) + slope_copies(batch, me, pair, 1):
            copy.start()
            started.append(copy)
    for batch in range(batches):
        for copy in slope_copies(batch, cross, me, 0):
            copy.wait_recv()
        for copy in slope_copies(batch, cross, pair, 2):
            copy.start()
            started.append(copy)
    for batch in range(batches):
        for copy in slope_copies(batch, pair, me, 1) + slope_copies(batch, far, me, 2):
            copy.wait_recv()
    for copy in started:
        copy.wait_send()


def col_exchange(partial):
    parts, batches, rows, lanes = partial.shape
    neg_rows = rows - 16
    vmem = pl.BlockSpec(memory_space=pltpu.VMEM)
    return pl.pallas_call(
        functools.partial(exchange_kernel, batches, neg_rows),
        out_shape=(
            jax.ShapeDtypeStruct((parts, batches, neg_rows, lanes), jnp.bfloat16),
            jax.ShapeDtypeStruct((parts, batches, 8, lanes), jnp.float32),
        ),
        in_specs=[vmem],
        out_specs=(vmem, vmem),
        scratch_shapes=[
            pltpu.VMEM((2, batches, rows, lanes), jnp.bfloat16),
            pltpu.VMEM((batches, rows, lanes), jnp.bfloat16),
            pltpu.VMEM((batches, rows, lanes), jnp.bfloat16),
            pltpu.SemaphoreType.DMA((2 * batches,)),
            pltpu.SemaphoreType.DMA((2 * batches,)),
            pltpu.SemaphoreType.DMA((batches,)),
            pltpu.SemaphoreType.DMA((batches,)),
            pltpu.SemaphoreType.DMA((3 * batches,)),
            pltpu.SemaphoreType.DMA((parts * batches,)),
            pltpu.SemaphoreType.DMA((3 * batches,)),
            pltpu.SemaphoreType.DMA((parts * batches,)),
        ],
        compiler_params=pltpu.CompilerParams(
            collective_id=0, has_side_effects=True, vmem_limit_bytes=48 * 1024 * 1024
        ),
    )(partial)


def shifted(shard, axis, by):
    size = lax.axis_size(axis)
    return lax.ppermute(shard, axis, [(i, (i + by) % size) for i in range(size)])


def gather_cols(table, indices):
    count = table.shape[1]
    one_hot = (
        lax.broadcasted_iota(jnp.int32, (count, indices.shape[0]), 0) == indices[None, :]
    ).astype(table.dtype)
    return jnp.dot(table, one_hot, preferred_element_type=jnp.float32)


def split_exact(values):
    high = values.astype(jnp.bfloat16)
    low = (values - high.astype(jnp.float32)).astype(jnp.bfloat16)
    return high, low


def scatter_rows(values, indices, count):
    one_hot = (
        lax.broadcasted_iota(jnp.int32, (count, indices.shape[0]), 0) == indices[None, :]
    ).astype(jnp.bfloat16)
    return lax.dot_general(
        one_hot, values, (((1,), (1,)), ((), ())), preferred_element_type=jnp.float32
    )


def scatter_f32(values, indices, count):
    rows = values.shape[0]
    high, low = split_exact(values)
    summed = scatter_rows(jnp.concatenate([high, low], axis=0), indices, count)
    return summed[:, :rows] + summed[:, rows:]


def body(embeddings, relations, source_ids, relation_ids, target_ids, negative_ids, served_rows):
    halves, columns, entities = embeddings.shape
    flat_width = halves * columns
    buckets, edge_count = source_ids.shape
    spans, negs_per = (negative_ids.shape[1], negative_ids.shape[2])
    span_len = edge_count // spans
    table = embeddings.reshape(flat_width, entities)
    relation_flat = relations.reshape(flat_width, relations.shape[2])
    served_flat = served_rows.reshape(-1)

    asked = [None] + [shifted(target_ids[b], "dom", -b) for b in range(1, buckets)]
    fetched = gather_cols(table, served_flat).astype(jnp.bfloat16)
    serving = [gather_cols(table, asked[b]).astype(jnp.bfloat16) for b in range(1, buckets)]
    table, *serving = lax.optimization_barrier((table, *serving))
    answered = [None] + [shifted(serving[b - 1], "dom", b) for b in range(1, buckets)]

    negative_pool = lax.all_to_all(
        fetched.reshape(halves, columns, -1), "dom", split_axis=2, concat_axis=2, tiled=True
    )
    pool_flat = negative_pool.reshape(flat_width, -1)
    pool_count = pool_flat.shape[1]

    def scores(bucket):
        negative_flat = negative_ids[bucket].reshape(-1)
        source_rows = gather_cols(table, source_ids[bucket]).reshape(halves, columns, edge_count)
        relation_rows = gather_cols(relation_flat, relation_ids[bucket]).reshape(
            halves, columns, edge_count
        )
        if bucket == 0:
            target_half = gather_cols(table, target_ids[0])
        else:
            target_half = answered[bucket].astype(jnp.float32)
        target_rows = target_half.reshape(halves, columns, edge_count)
        product = jnp.stack(
            [
                source_rows[0] * relation_rows[0] - source_rows[1] * relation_rows[1],
                source_rows[0] * relation_rows[1] + source_rows[1] * relation_rows[0],
            ]
        )
        rounded = product.astype(jnp.bfloat16)
        rounded_wide = rounded.astype(jnp.float32)
        positive_part = jnp.sum(rounded_wide * target_rows, axis=(0, 1))
        negative_rows = gather_cols(pool_flat, negative_flat).astype(jnp.bfloat16).reshape(
            flat_width, spans, negs_per
        )
        query_rows = rounded.reshape(flat_width, spans, span_len)
        negative_part = lax.dot_general(
            query_rows,
            negative_rows,
            (((0,), (0,)), ((1,), (1,))),
            preferred_element_type=jnp.float32,
        ).reshape(spans, -1, 128)
        positive_rows = positive_part.reshape(spans, -1, 128)
        pad = jnp.zeros((spans, 16 - positive_rows.shape[1], 128), jnp.float32)
        partial = jnp.concatenate([negative_part, positive_rows, pad], axis=1).astype(
            jnp.bfloat16
        )
        state = (relation_rows, target_rows, rounded, rounded_wide, negative_rows, query_rows)
        return partial, state

    def gradients(bucket, reduced, state):
        relation_rows, target_rows, rounded, rounded_wide, negative_rows, query_rows = state
        negative_slope, positive_sums = reduced
        positive = positive_sums[:, : span_len // 128].reshape(edge_count)
        positive_slope = -jax.nn.sigmoid(-positive)
        slope_spans = negative_slope.reshape(spans, span_len, negs_per)
        pool_terms = lax.dot_general(
            query_rows,
            slope_spans,
            (((2,), (1,)), ((1,), (0,))),
            preferred_element_type=jnp.float32,
        ).transpose(1, 0, 2).reshape(flat_width, spans * negs_per)
        query_terms = lax.dot_general(
            slope_spans,
            negative_rows,
            (((2,), (2,)), ((0,), (1,))),
            preferred_element_type=jnp.float32,
        )
        query_terms = query_terms.transpose(2, 0, 1).reshape(halves, columns, edge_count)
        total_grad = positive_slope * target_rows + query_terms
        target_values = (positive_slope * rounded_wide).reshape(flat_width, edge_count)
        source_grad = jnp.stack(
            [
                total_grad[0] * relation_rows[0] + total_grad[1] * relation_rows[1],
                total_grad[1] * relation_rows[0] - total_grad[0] * relation_rows[1],
            ]
        ).reshape(flat_width, edge_count)
        return pool_terms, target_values, source_grad

    owned = jnp.zeros((entities, flat_width), jnp.float32)
    pool_values, pool_index = [], []
    bf16_values, bf16_index = [], []
    results = [scores(bucket) for bucket in range(buckets)]
    negative_all, positive_all = col_exchange(jnp.stack([r[0] for r in results], axis=1))
    for done in range(buckets):
        reduced = (negative_all[:, done], positive_all[:, done])
        pool_terms, target_values, source_grad = gradients(done, reduced, results[done][1])
        pool_values.append(pool_terms)
        pool_index.append(negative_ids[done].reshape(-1))
        if done == 0:
            owned = owned + scatter_f32(
                jnp.concatenate([source_grad, target_values], axis=1),
                jnp.concatenate([source_ids[0], target_ids[0]]),
                entities,
            )
        else:
            owned = owned + scatter_f32(source_grad, source_ids[done], entities)
            bf16_values.append(shifted(target_values.astype(jnp.bfloat16), "dom", -done))
            bf16_index.append(asked[done])

    pool_grad = scatter_f32(
        jnp.concatenate(pool_values, axis=1), jnp.concatenate(pool_index), pool_count
    ).T
    returned = lax.all_to_all(
        pool_grad.reshape(halves, columns, -1).astype(jnp.bfloat16),
        "dom",
        split_axis=2,
        concat_axis=2,
        tiled=True,
    ).reshape(flat_width, -1)
    bf16_values.append(returned)
    bf16_index.append(served_flat)
    owned = owned + scatter_rows(
        jnp.concatenate(bf16_values, axis=1), jnp.concatenate(bf16_index), entities
    )
    return owned.T.reshape(halves, columns, entities)


def solution(mesh):
    placed = (
        P(None, "col", "dom"),
        P(None, "col", None),
        P(None, "dom"),
        P(None, "dom"),
        P(None, "dom"),
        P(None, "dom", None),
        P("dom", None),
    )
    return jax.shard_map(
        body, mesh=mesh, in_specs=placed, out_specs=P(None, "col", "dom"), check_vma=False
    )
```
